32 devices in a mesh: dp: 8 (over z, core), seq: 4 (over y, x).
Axes of the slice: x: 2, y: 2, z: 4, core: 2. Of those that a mesh axis runs over, the one named last changes fastest.
Arguments:
- tokens: int32 [8, 65536], P('dp', 'seq'), may hold values from 0 to 4
- stem_weight: bfloat16 [60, 768], replicated, may hold values from -1.5 to 1.5
- stem_bias: float32 [768], replicated, may hold values from -3 to 3
- conv_gain: float32 [768], replicated, may hold values from 0.1 to 1.9
- conv_weight: bfloat16 [5, 768, 1536], P(None, 'dp'), may hold values from -0.09375 to 0.09375
- conv_bias: float32 [1536], replicated, may hold values from -3 to 3
- attn_gain: float32 [1536], replicated, may hold values from 0.1 to 1.9
- w_query: bfloat16 [1536, 1024], P('dp'), may hold values from -7 to 7
- w_key: bfloat16 [1536, 128], P('dp'), may hold values from -0.15625 to 0.15625
- w_value: bfloat16 [1536, 192], P('dp'), may hold values from -0.15625 to 0.15625
- w_out: bfloat16 [1536, 1536], P('dp'), may hold values from -0.4375 to 0.4375
Outputs:
- features: bfloat16 [8, 512, 1536], P('dp', 'seq')
The draws below stay inside these ranges and needn't reach their ends.
Inputs may be any that keep to these rules, and one draw needn't show every extreme that they name: `tokens`: 0 is an unknown base; 1 to 4 are A, C, G, T.
All inputs are finite; a program needn't handle non-finite values.
Results may differ from the reference program's by a relative error of at most 0.009.
The reference program's roundings to bfloat16 on the way count: a program that leaves them out, or rounds other values in their place, can miss the bound.
Values may be sent and summed in bfloat16 or wider, within the bound.
A program may use at most 192 MiB of HBM per device.

```python
import math
import jax
import jax.numpy as jnp
from jax import lax

D_STEM = 768
D = 1536
HEADS = 8
HEAD_K = 128
HEAD_V = 192
KW_STEM = 15
KW = 5
POOL_A = 8
POOL_B = 16
STEM_IN = 60
LENGTH = 65536
POSITIONS = 512
WINDOWS = 8


def draw_w_query(key, part):
    normal_part = jnp.clip(jax.random.normal(key, (D, HEADS * HEAD_K), jnp.float32), -4.0, 4.0) * (1.0 / math.sqrt(D))
    return normal_part.astype(jnp.bfloat16)


def with_ends(drawn, rng, smallest, largest):
    extent = drawn.shape
    spot = [jax.random.randint(jax.random.fold_in(rng, axis), (), 0, extent[axis]) for axis in range(len(extent))]
    drawn = drawn.at[tuple(spot)].set(smallest)
    longest = extent.index(max(extent))
    spot[longest] = (spot[longest] + 1) % extent[longest]
    return drawn.at[tuple(spot)].set(largest)


def level_of(key, extent, split, least, high):
    def one(dim, blocks):
        draws = jax.random.uniform(jax.random.fold_in(jax.random.fold_in(key, 6), dim), (blocks,), jnp.float32, least / len(split), high / len(split))
        return jnp.repeat(jnp.exp(draws), extent[dim] // blocks).reshape((-1,) + (1,) * (len(extent) - dim - 1))

    loudness = one(*split[0])
    for cut in split[1:]:
        loudness = loudness * one(*cut)
    return loudness


def normal_values(own_key, shape, spread, most, cuts=(), held_as=jnp.bfloat16):
    level = level_of(own_key, shape, cuts, -0.22, 0.18) if cuts else 1.0
    array = jax.random.normal(own_key, shape, jnp.float32) * spread * level
    return jnp.minimum(jnp.maximum(array, -most), most).astype(held_as)


def setup_inputs(seed: int = 0) -> dict:
    streams_of = jax.random.split(jax.random.key(seed), 12)
    tokens = with_ends(jax.random.randint(streams_of[0], (WINDOWS, LENGTH), 0, 5), jax.random.fold_in(streams_of[0], 1), 0, 4).astype(jnp.int32)
    stem_weight = normal_values(streams_of[1], (STEM_IN, D_STEM), KW_STEM ** -0.5, 1.5)
    stem_bias = normal_values(streams_of[2], (D_STEM,), 0.5, 3.0, (), jnp.float32)
    conv_gain = jnp.clip(1.0 + 0.18 * jax.random.normal(streams_of[3], (D_STEM,), jnp.float32), 0.1, 1.9)
    conv_weight = normal_values(streams_of[4], (KW, D_STEM, D), (KW * D_STEM) ** -0.5, 0.09375, ((1, 8),))
    conv_bias = normal_values(streams_of[5], (D,), 0.5, 3.0, (), jnp.float32)
    attn_gain = jnp.clip(1.0 + 0.18 * jax.random.normal(streams_of[6], (D,), jnp.float32), 0.1, 1.9)
    w_query = draw_w_query(jax.random.fold_in(streams_of[11], 71), 0)
    w_key = normal_values(streams_of[8], (D, HEAD_K), D ** -0.5, 0.15625, ((0, 8),))
    w_value = normal_values(streams_of[9], (D, HEAD_V), D ** -0.5, 0.15625, ((0, 8),))
    w_out = normal_values(streams_of[10], (HEADS * HEAD_V, D), HEAD_V ** -0.5, 0.4375, ((0, 8),))
    return {"tokens": tokens, "stem_weight": stem_weight, "stem_bias": stem_bias, "conv_gain": conv_gain, "conv_weight": conv_weight, "conv_bias": conv_bias, "attn_gain": attn_gain, "w_query": w_query, "w_key": w_key, "w_value": w_value, "w_out": w_out}


epsilon = 1e-06

def stem_pool(padded_tokens, count, stem_weight, stem_bias):
    columns = jnp.stack([padded_tokens[offset:offset + count] for offset in range(KW_STEM)], axis=1)
    codes = jnp.arange(1, 5, dtype=jnp.int32)
    onehot = (columns[:, :, None] == codes).astype(jnp.bfloat16).reshape(count, KW_STEM * 4)
    block_len = min(count, 1024)
    onehot = onehot.reshape(count // block_len, block_len, KW_STEM * 4)

    def one_block(inputs):
        stem_rows = jnp.dot(inputs, stem_weight, preferred_element_type=jnp.float32) + stem_bias
        return jax.nn.gelu(lax.optimization_barrier(jnp.max(stem_rows.reshape(block_len // POOL_A, POOL_A, -1), axis=1)))
    return lax.map(one_block, onehot).reshape(count // POOL_A, -1).astype(jnp.bfloat16)

def rms_scale(values, gain):
    return values * lax.rsqrt(lax.optimization_barrier(jnp.mean(values * values, axis=-1, keepdims=True)) + epsilon) * gain

def rotate(values, angles):
    half_dim = values.shape[-1] // 2
    first = values[..., :half_dim]
    second = values[..., half_dim:]
    cosine = jnp.cos(angles)
    sine = jnp.sin(angles)
    return jnp.concatenate([first * cosine - second * sine, second * cosine + first * sine], axis=-1)

def reference(tokens, stem_weight, stem_bias, conv_gain, conv_weight, conv_bias, attn_gain, w_query, w_key, w_value, w_out):
    reach = KW_STEM // 2
    edge_rows = KW // 2

    def one_window(window_tokens):
        padded_tokens = jnp.pad(window_tokens, (reach, reach))
        pooled = stem_pool(padded_tokens, LENGTH, stem_weight, stem_bias)
        normed = rms_scale(pooled.astype(jnp.float32), conv_gain).astype(jnp.bfloat16)
        row_count = LENGTH // POOL_A
        padded_rows = jnp.pad(normed, ((edge_rows, edge_rows), (0, 0)))
        conv_sum = jnp.zeros((row_count, D), jnp.float32) + conv_bias
        for offset in range(KW):
            conv_sum = conv_sum + jnp.dot(padded_rows[offset:offset + row_count], conv_weight[offset], preferred_element_type=jnp.float32)
        coarse = lax.optimization_barrier(jnp.max(jax.nn.gelu(conv_sum).reshape(row_count // POOL_B, POOL_B, D), axis=1)).astype(jnp.bfloat16)
        residual = coarse.astype(jnp.float32)
        hidden = rms_scale(residual, attn_gain).astype(jnp.bfloat16)
        query = jnp.dot(hidden, w_query, preferred_element_type=jnp.float32).reshape(POSITIONS, HEADS, HEAD_K)
        keys = jnp.dot(hidden, w_key, preferred_element_type=jnp.float32)
        values = jnp.dot(hidden, w_value, preferred_element_type=jnp.float32).astype(jnp.bfloat16)
        half_dim = HEAD_K // 2
        freqs = 10000.0 ** (-jnp.arange(half_dim, dtype=jnp.float32) / half_dim)
        angles = jnp.arange(POSITIONS, dtype=jnp.int32).astype(jnp.float32)[:, None] * freqs[None, :]
        query = rotate(query, angles[:, None, :]).astype(jnp.bfloat16)
        keys = rotate(keys, angles).astype(jnp.bfloat16)
        scores = jnp.einsum('rhd,kd->hrk', query.astype(jnp.float32), keys.astype(jnp.float32)) * HEAD_K ** (-0.5)
        weights = jax.nn.softmax(scores, axis=-1).astype(jnp.bfloat16)
        mixed = jnp.einsum('hrk,kd->rhd', weights.astype(jnp.float32), values.astype(jnp.float32)).astype(jnp.bfloat16)
        mixed = mixed.reshape(POSITIONS, HEADS * HEAD_V)
        return (residual + jnp.dot(mixed, w_out, preferred_element_type=jnp.float32)).astype(jnp.bfloat16)
    return lax.map(one_window, tokens)
```

```python
import functools

import jax
import jax.numpy as jnp
from jax import lax
from jax.experimental import pallas as pl
from jax.experimental.pallas import tpu as pltpu
from jax.sharding import PartitionSpec as P

HEADS = 8
HEAD_K = 128
HEAD_V = 192
KW_STEM = 15
KW = 5
POOL_A = 8
POOL_B = 16
GROUP = POOL_A * POOL_B
SPAN = 24

epsilon = 1e-06


def rms_scale(values, gain):
    return values * lax.rsqrt(jnp.mean(values * values, axis=-1, keepdims=True) + epsilon) * gain


def rotate(values, angles):
    half_dim = values.shape[-1] // 2
    first = values[..., :half_dim]
    second = values[..., half_dim:]
    cosine = jnp.cos(angles)
    sine = jnp.sin(angles)
    return jnp.concatenate(
        [first * cosine - second * sine, second * cosine + first * sine], axis=-1
    )


def stem_kernel(
    tok_ref, low_ref, high_ref, weight_ref, bias_ref, gain_ref, ext_ref, text_ref, hot_ref, shifted_ref, rows_ref
):
    stem_compute(
        tok_ref,
        low_ref[...],
        high_ref[...],
        weight_ref,
        bias_ref,
        gain_ref,
        ext_ref,
        text_ref,
        hot_ref,
        shifted_ref,
        rows_ref,
    )


def stem_shift(weight_ref, shifted_ref):
    source = lax.broadcasted_iota(jnp.int32, (GROUP, weight_ref.shape[0]), 1)
    target = lax.broadcasted_iota(jnp.int32, (GROUP, weight_ref.shape[0]), 0)
    tap = source // 4
    base = source - 4 * tap
    for offset in range(POOL_A):
        pick = (target == base * SPAN + offset + tap + 1).astype(jnp.float32).astype(jnp.bfloat16)
        shifted_ref[offset] = jnp.dot(
            pick, weight_ref[...], preferred_element_type=jnp.float32
        ).astype(jnp.bfloat16)


def stem_tokens(tok_ref, low, high, text_ref, hot_ref):
    count = tok_ref.shape[0]
    main = tok_ref[...].astype(jnp.float32)
    row = lax.broadcasted_iota(jnp.int32, main.shape, 0)
    previous = jnp.where(row == 0, low.astype(jnp.float32), pltpu.roll(main, 1, 0))
    following = jnp.where(
        row == count - 1, high.astype(jnp.float32), pltpu.roll(main, count - 1, 0)
    )
    text_ref[0:SPAN, :] = previous.T[GROUP - SPAN :, :]
    text_ref[SPAN : SPAN + GROUP, :] = main.T
    text_ref[SPAN + GROUP :, :] = following.T[:SPAN, :]

    def hot_of(span):
        planes = [(span == float(code)).astype(jnp.float32) for code in range(1, 5)]
        planes.append(jnp.zeros((GROUP - 4 * SPAN, span.shape[1]), jnp.float32))
        return jnp.concatenate(planes, axis=0).T.astype(jnp.bfloat16)

    for j in range(POOL_B):
        hot_ref[j] = hot_of(text_ref[8 * j + SPAN - 8 : 8 * j + 2 * SPAN - 8, :])
    lane = lax.broadcasted_iota(jnp.int32, (SPAN, count), 1)
    edge = jnp.where(
        lane == 0,
        text_ref[0:SPAN, :],
        jnp.where(
            lane == 1,
            pltpu.roll(text_ref[8 : 8 + SPAN, :], 1, 1),
            jnp.where(
                lane == 2,
                pltpu.roll(text_ref[GROUP + SPAN - 8 : GROUP + 2 * SPAN - 8, :], 3, 1),
                pltpu.roll(text_ref[GROUP + SPAN : GROUP + 2 * SPAN, :], 4, 1),
            ),
        ),
    )
    hot_ref[POOL_B] = hot_of(edge)


def stem_block(j, bias_ref, gain_ref, ext_ref, hot_ref, shifted_ref, rows_ref):
    count, channels = rows_ref.shape
    width = 256
    hot = hot_ref[j]
    for chunk in range(channels // width):
        columns = slice(chunk * width, (chunk + 1) * width)
        best = None
        for offset in range(POOL_A):
            stem = jnp.dot(hot, shifted_ref[offset, :, columns], preferred_element_type=jnp.float32)
            best = stem if best is None else jnp.maximum(best, stem)
        pooled = jax.nn.gelu(best + bias_ref[:, columns]).astype(jnp.bfloat16)
        rows_ref[:, columns] = pooled.astype(jnp.float32)
    pooled = rows_ref[...]
    start = pl.multiple_of((j + 2) * count, count)
    ext_ref[pl.ds(start, count), :] = rms_scale(pooled, gain_ref[...]).astype(jnp.bfloat16)


def stem_edges(place, last_place, ext_ref, rows_ref):
    count, channels = rows_ref.shape
    edges = ext_ref[(POOL_B + 2) * count : (POOL_B + 3) * count, :].astype(jnp.float32)
    left_keep = (place > 0).astype(jnp.float32)
    right_keep = (place < last_place).astype(jnp.float32)
    spot = lax.broadcasted_iota(jnp.int32, (count, channels), 0)
    for index in range(2):
        inner = ext_ref[(POOL_B + index) * count : (POOL_B + index + 1) * count, :]
        moved = pltpu.roll(inner.astype(jnp.float32), 1, 0)
        ext_ref[index * count : (index + 1) * count, :] = jnp.where(
            spot == 0, edges[index : index + 1, :] * left_keep, moved
        ).astype(jnp.bfloat16)
        inner = ext_ref[(2 + index) * count : (3 + index) * count, :]
        moved = pltpu.roll(inner.astype(jnp.float32), count - 1, 0)
        at = POOL_B + 2 + index
        ext_ref[at * count : (at + 1) * count, :] = jnp.where(
            spot == count - 1, edges[2 + index : 3 + index, :] * right_keep, moved
        ).astype(jnp.bfloat16)


def stem_compute(
    tok_ref, low, high, weight_ref, bias_ref, gain_ref, ext_ref, text_ref, hot_ref, shifted_ref, rows_ref
):
    stem_shift(weight_ref, shifted_ref)
    stem_tokens(tok_ref, low, high, text_ref, hot_ref)

    def block(j, carry):
        stem_block(j, bias_ref, gain_ref, ext_ref, hot_ref, shifted_ref, rows_ref)
        return carry

    lax.fori_loop(0, POOL_B + 1, block, 0)
    stem_edges(lax.axis_index("seq"), lax.axis_size("seq") - 1, ext_ref, rows_ref)


def stem_stage(tokens, low, high, stem_weight, stem_bias, conv_gain):
    count = tokens.shape[0]
    channels = stem_weight.shape[1]
    return pl.pallas_call(
        stem_kernel,
        out_shape=jax.ShapeDtypeStruct(((POOL_B + 4) * count, channels), jnp.bfloat16),
        in_specs=[pl.BlockSpec(memory_space=pltpu.VMEM)] * 6,
        out_specs=pl.BlockSpec(memory_space=pltpu.VMEM),
        scratch_shapes=[
            pltpu.VMEM((GROUP + 2 * SPAN, count), jnp.float32),
            pltpu.VMEM((POOL_B + 1, count, GROUP), jnp.bfloat16),
            pltpu.VMEM((POOL_A, GROUP, channels), jnp.bfloat16),
            pltpu.VMEM((count, channels), jnp.float32),
        ],
        cost_estimate=pl.CostEstimate(
            flops=20_000_000_000, bytes_accessed=4_000_000, transcendentals=1_600_000
        ),
        name="stem_stage",
    )(tokens, low, high, stem_weight, stem_bias[None], conv_gain[None])


def conv_kernel(count, ext_ref, weight_ref, bias_ref, coarse_ref):
    group = 4
    width = weight_ref.shape[-1]
    channels = ext_ref.shape[1]

    def block(m, carry):
        most, least = carry
        total = None
        for tap in range(KW):
            start = pl.multiple_of((m * group + tap) * count, count)
            part = jnp.dot(
                ext_ref[pl.ds(start, group * count), :],
                weight_ref[:, :, 0, tap].reshape(channels, width),
                preferred_element_type=jnp.float32,
            )
            total = part if total is None else total + part
        for index in range(group):
            piece = total[index * count : (index + 1) * count]
            most = jnp.maximum(most, piece)
            least = jnp.minimum(least, piece)
        return most, least

    big = jnp.full((count, width), jnp.finfo(jnp.float32).max, jnp.float32)
    most, least = lax.fori_loop(0, POOL_B // group, block, (-big, big))
    bias = bias_ref[...]
    coarse_ref[...] = jnp.maximum(jax.nn.gelu(most + bias), jax.nn.gelu(least + bias)).astype(
        jnp.bfloat16
    )


def conv_stage(ext, weight, conv_bias):
    count = ext.shape[0] // (POOL_B + 4)
    ways, row_parts, column_parts, taps, depth, columns = weight.shape
    width = 256
    steps = columns // width
    return pl.pallas_call(
        functools.partial(conv_kernel, count),
        grid=(column_parts, steps),
        out_shape=jax.ShapeDtypeStruct((count, column_parts * columns), jnp.bfloat16),
        in_specs=[
            pl.BlockSpec(ext.shape, lambda b, n: (0, 0), pipeline_mode=pl.Buffered(1)),
            pl.BlockSpec(
                (ways, row_parts, 1, taps, depth, width), lambda b, n: (0, 0, b, 0, 0, n)
            ),
            pl.BlockSpec((1, width), lambda b, n: (0, b * steps + n)),
        ],
        out_specs=pl.BlockSpec((count, width), lambda b, n: (0, b * steps + n)),
        cost_estimate=pl.CostEstimate(
            flops=24_000_000_000, bytes_accessed=16_000_000, transcendentals=400_000
        ),
        name="conv_stage",
    )(ext, weight, conv_bias[None])


MESH = pl.DeviceIdType.MESH


UNITS = 12


def encoder_kernel(
    tok_ref,
    stem_weight_ref,
    stem_bias_ref,
    gain_ref,
    conv_bias_ref,
    attn_gain_ref,
    cosine_ref,
    sine_ref,
    conv_ref,
    query_ref,
    keyw_ref,
    valuew_ref,
    outw_ref,
    out_ref,
    coarse_ref,
    key_ref,
    value_ref,
    text_ref,
    hot_ref,
    shifted_ref,
    rows_ref,
    ext_ref,
    low_ref,
    high_ref,
    conv_full,
    proj_full,
    outw_full,
    pair_send,
    pair_recv,
    halo_send,
    halo_recv,
    local_sem,
    recv_sem,
    panel_sem,
    partner_sem,
    x_sem,
    y_sem,
    partner_send,
    own_sem,
    relay_sem,
):
    wide = out_ref.shape[1]
    members = lax.axis_size("seq")
    me = lax.axis_index("dp")
    place = lax.axis_index("seq")
    chip = me // 2
    core = me % 2
    chips = lax.axis_size("dp") // 2
    partner = (chip * 2 + 1 - core, place)
    count = tok_ref.shape[0]
    depth = conv_full.shape[3]
    unit_cols = conv_full.shape[4]
    unit_rows = proj_full.shape[1] // UNITS
    split = HEADS * HEAD_K
    middle = split + HEAD_K

    along_x = place + 1 - 2 * (place % 2)
    along_y = place + 2 - 4 * (place // 2)
    across = 3 - place
    mine = (place % 2 + place // 2) % 2
    theirs = 1 - mine
    x_target = (me, along_x)
    y_target = (me, along_y)

    sources = (1 + chip % 2, (chip + 2) % chips, 3 - 3 * (chip % 2))
    inner = (chip > 0) & (chip < chips - 1)
    relays = (3 * (chip - 1), None, chips - 1 - chip)

    z_units = (2 * place, 2 * place + 1, 8 + 2 * mine, 9 + 2 * mine)
    x_out = (2 * place, 2 * place + 1, 2 * along_y + 1, 8 + 2 * mine)
    y_out = (2 * place, 2 * place + 1, 2 * along_x, 9 + 2 * mine)
    x_in = (2 * along_x, 2 * along_x + 1, 2 * across + 1, 8 + 2 * theirs)
    y_in = (2 * along_y, 2 * along_y + 1, 2 * across, 9 + 2 * theirs)

    def part(kind, way, unit, span):
        if kind == 0:
            return conv_full.at[way, pl.ds(unit, span)]
        full = proj_full if kind == 1 else outw_full
        return full.at[way, pl.ds(pl.multiple_of(unit * unit_rows, unit_rows), span * unit_rows)]

    def z_message(kind, i):
        return (z_units[i], 1) if kind == 0 else (z_units[2 * i], 2)

    def plane_messages(kind, i):
        if kind == 0:
            return ((i, 1),)
        return ((0, 2),) if i == 0 else ((2, 1), (3, 1))

    def remote(ref, send_sem, recv, target):
        return pltpu.make_async_remote_copy(ref, ref, send_sem, recv, target, MESH)

    def arrived(ref, recv):
        remote(ref, x_sem.at[0], recv, partner).wait_recv()

    def to_partner(kind, way, unit, span):
        recv = panel_sem.at[unit // 2] if kind == 0 else partner_sem.at[kind]
        remote(part(kind, way, unit, span), partner_send.at[kind], recv, partner).start()

    def own(kind, i):
        ref = part(kind, me, *z_message(kind, i))
        recv = recv_sem.at[kind, chip, i]

        @pl.when(chip < chips - 1)
        def _():
            remote(ref, own_sem.at[kind, 0], recv, (me + 2, place)).start()

        @pl.when(chip > 0)
        def _():
            remote(ref, own_sem.at[kind, 1], recv, (me - 2, place)).start()

        @pl.when(jnp.logical_not(inner))
        def _():
            far = 2 * (chips - 1 - chip) + core
            remote(ref, own_sem.at[kind, 2], recv, (far, place)).start()

    def z_step(kind, i, j):
        origin = sources[j]
        way = 2 * origin + core
        unit, span = z_message(kind, i)
        ref = part(kind, way, unit, span)
        recv = recv_sem.at[kind, origin, i]
        arrived(ref, recv)
        if relays[j] is not None:

            @pl.when(inner)
            def _():
                remote(ref, relay_sem.at[kind, j // 2], recv, (2 * relays[j] + core, place)).start()

        for k, width in plane_messages(kind, i):
            for base, units, sem, target in ((4, x_out, x_sem, x_target), (8, y_out, y_sem, y_target)):
                recv = recv_sem.at[kind, origin, base + k]
                remote(part(kind, way, units[k], width), sem.at[kind], recv, target).start()
        to_partner(kind, way, unit, span)

    def plane_step(kind, i, j):
        origin = sources[j]
        way = 2 * origin + core
        for k, width in plane_messages(kind, i):
            for base, units in ((4, x_in), (8, y_in)):
                arrived(part(kind, way, units[k], width), recv_sem.at[kind, origin, base + k])
                to_partner(kind, way, units[k], width)

    stream = ((0, 0), (0, 1), (0, 2), (0, 3), (1, 0), (1, 1), (2, 0), (2, 1))
    events = []
    for turn in range(len(stream) + 1):
        for j in range(3):
            at = turn - (j == 1)
            if 0 <= at < len(stream) and not (turn == len(stream) and j != 1):
                events.append((at, j))
    lag = 2

    def event(n):
        def plane():
            if lag <= n < len(events) + lag:
                at, j = events[n - lag]
                plane_step(*stream[at], j)

        last = n == len(events) - 1
        if last:
            plane()
        if n < len(events):
            at, j = events[n]
            z_step(*stream[at], j)
            if j == 2 and at + 2 < len(stream):
                own(*stream[at + 2])
        if not last:
            plane()

    def event_of(number, first, last):
        for n in range(first, last):

            @pl.when(number == n - first)
            def _():
                event(n)

    def local_copies(kind):
        if kind == 0:
            for unit in range(UNITS):
                yield conv_ref.at[:, :, pl.ds(unit * unit_cols, unit_cols)], conv_full.at[me, unit]
        elif kind == 1:
            yield query_ref, proj_full.at[me, :, pl.ds(0, split)]
            yield keyw_ref, proj_full.at[me, :, pl.ds(split, HEAD_K)]
            yield valuew_ref, proj_full.at[me, :, pl.ds(middle, HEAD_V)]
        else:
            yield outw_ref, outw_full.at[me]

    def local_start(kind):
        for a, b in local_copies(kind):
            pltpu.make_async_copy(a, b, local_sem.at[kind]).start()

    def local_wait(kind):
        whole = (conv_full, proj_full, outw_full)[kind].at[me]
        pltpu.make_async_copy(whole, whole, local_sem.at[kind]).wait()

    def own_partner(kind):
        if kind == 0:
            for panel in range(UNITS // 2):
                to_partner(0, me, 2 * panel, 2)
        else:
            to_partner(kind, me, 0, UNITS)

    local_start(0)
    barrier = pltpu.get_barrier_semaphore()
    pl.semaphore_signal(barrier, inc=1, device_id=partner, device_id_type=MESH)
    for turn in range(1, members):
        pl.semaphore_signal(
            barrier, inc=1, device_id=(me, (place + turn) % members), device_id_type=MESH
        )

    for turn in (1, chips - 1):
        neighbour = (chip + turn) % chips * 2 + core
        pl.semaphore_signal(barrier, inc=1, device_id=(neighbour, place), device_id_type=MESH)
    local_start(1)
    local_start(2)
    local_wait(0)
    pl.semaphore_wait(barrier, members + 2)

    own(0, 0)
    own(0, 1)
    right = (place + 1) % members
    left = (place + members - 1) % members
    halo = [
        pltpu.make_async_remote_copy(
            tok_ref.at[count - 8 : count], low_ref, halo_send.at[0], halo_recv.at[0], (me, right), MESH
        ),
        pltpu.make_async_remote_copy(
            tok_ref.at[0:8], high_ref, halo_send.at[1], halo_recv.at[1], (me, left), MESH
        ),
    ]
    for copy in halo:
        copy.start()
    own_partner(0)
    local_wait(1)
    own_partner(1)
    local_wait(2)
    own_partner(2)
    stem_shift(stem_weight_ref, shifted_ref)
    for copy in halo:
        copy.wait()
    low = jnp.where(place > 0, low_ref[7:8], 0)
    high = jnp.where(place < members - 1, high_ref[0:1], 0)
    stem_tokens(tok_ref, low, high, text_ref, hot_ref)

    def stem_round(r, nothing):
        def block(j, nothing):
            stem_block(j, stem_bias_ref, gain_ref, ext_ref, hot_ref, shifted_ref, rows_ref)
            return nothing

        lax.fori_loop(3 * r - (r + 5) // 6, 3 * r + 2, block, 0)
        event_of(r, 0, 6)
        return nothing

    lax.fori_loop(0, (POOL_B + 2) // 3, stem_round, 0)
    stem_edges(place, members - 1, ext_ref, rows_ref)
    event(6)

    width = 2 * unit_cols
    group = 8
    channels = ext_ref.shape[1]
    big = jnp.full((count, width), jnp.finfo(jnp.float32).max, jnp.float32)

    def conv_panel(panel, after):
        block_of = pl.ds(0, chips)
        whole = conv_full.at[block_of, pl.ds(0, 2)]
        arrived(whole, panel_sem.at[panel])

        def block(m, carry):
            most, least = carry
            total = None
            for tap in range(KW):
                start = pl.multiple_of((m * group + tap) * count, count)
                weight = jnp.concatenate(
                    [conv_full[:, 2 * panel + h, tap].reshape(channels, unit_cols) for h in range(2)], axis=1
                )
                piece = jnp.dot(
                    ext_ref[pl.ds(start, group * count), :], weight, preferred_element_type=jnp.float32
                )
                total = piece if total is None else total + piece
            for index in range(group):
                piece = total[index * count : (index + 1) * count]
                most = jnp.maximum(most, piece)
                least = jnp.minimum(least, piece)
            after(m)
            return most, least

        most, least = lax.fori_loop(0, POOL_B // group, block, (-big, big))
        at = pl.multiple_of(panel * width, width)
        bias = conv_bias_ref[:, pl.ds(at, width)]
        coarse_ref[:, pl.ds(at, width)] = jnp.maximum(
            jax.nn.gelu(most + bias), jax.nn.gelu(least + bias)
        ).astype(jnp.bfloat16)

    def conv_turn(t, nothing):
        plane = (place % 2 + t % 2) % 2 + 2 * ((place // 2 + t // 2) % 2)
        shared = t // 4
        panel = (1 - shared) * plane + shared * (4 + (mine + t) % 2)
        conv_panel(panel, lambda m: event_of(2 * t + m, 7, 19))
        return nothing

    lax.fori_loop(0, UNITS // 2, conv_turn, 0)
    event(19)
    event(20)
    arrived(proj_full.at[pl.ds(0, chips)], partner_sem.at[1])

    def weight(begin, end):
        return proj_full[:, :, begin:end].reshape(wide, end - begin)

    cosine = jnp.concatenate([cosine_ref[...], cosine_ref[...]], axis=1)
    sine = jnp.concatenate([-sine_ref[...], sine_ref[...]], axis=1)

    def turned(head):
        return (head * cosine + pltpu.roll(head, HEAD_K // 2, 1) * sine).astype(jnp.bfloat16)

    hidden = rms_scale(coarse_ref[...].astype(jnp.float32), attn_gain_ref[...]).astype(
        jnp.bfloat16
    )
    key_ref[place] = turned(
        jnp.dot(hidden, weight(split, middle), preferred_element_type=jnp.float32)
    )
    value_ref[place] = jnp.dot(
        hidden, weight(middle, middle + HEAD_V), preferred_element_type=jnp.float32
    ).astype(jnp.bfloat16)
    pairs = []
    for turn in range(1, members):
        for index, ref in enumerate((key_ref, value_ref)):
            copy = pltpu.make_async_remote_copy(
                ref.at[place],
                ref.at[place],
                pair_send.at[index, turn],
                pair_recv.at[index, place],
                (me, (place + turn) % members),
                MESH,
            )
            copy.start()
            pairs.append(copy)
    query = jnp.dot(hidden, weight(0, split), preferred_element_type=jnp.float32)
    event(21)
    for turn in range(1, members):
        spot = (place + turn) % members
        for index, ref in enumerate((key_ref, value_ref)):
            arrived(ref.at[spot], pair_recv.at[index, spot])
    keys = key_ref[...].reshape(members * count, HEAD_K)
    values = value_ref[...].reshape(members * count, HEAD_V)
    mixes = []
    for head in range(HEADS):
        scores = lax.dot_general(
            turned(query[:, head * HEAD_K : (head + 1) * HEAD_K]),
            keys,
            (((1,), (1,)), ((), ())),
            preferred_element_type=jnp.float32,
        ) * HEAD_K ** (-0.5)
        raised = jnp.exp(scores - jnp.max(scores, axis=-1, keepdims=True))
        weights = (raised / jnp.sum(raised, axis=-1, keepdims=True)).astype(jnp.bfloat16)
        mixes.append(
            jnp.dot(weights, values, preferred_element_type=jnp.float32).astype(jnp.bfloat16)
        )
        if head in (3, 7):
            event(22 + head // 4)
    for n in range(24, len(events) + lag):
        event(n)
    arrived(outw_full.at[pl.ds(0, chips)], partner_sem.at[2])
    total = coarse_ref[...].astype(jnp.float32)
    for head in range(HEADS):
        total = total + jnp.dot(mixes[head], outw_full[head], preferred_element_type=jnp.float32)
    out_ref[...] = total.astype(jnp.bfloat16)
    for copy in pairs:
        copy.wait_send()
    for kind, full in enumerate((conv_full, proj_full, outw_full)):
        whole = full.at[0]
        remote(whole, x_sem.at[kind], recv_sem.at[0, 0, 0], x_target).wait_send()
        remote(whole, y_sem.at[kind], recv_sem.at[0, 0, 0], y_target).wait_send()
        every = full.at[pl.ds(0, chips)]
        remote(every, partner_send.at[kind], recv_sem.at[0, 0, 0], partner).wait_send()
        ref = part(kind, 0, 0, 4)

        @pl.when(chip < chips - 1)
        def _():
            remote(ref, own_sem.at[kind, 0], recv_sem.at[0, 0, 0], partner).wait_send()

        @pl.when(chip > 0)
        def _():
            remote(ref, own_sem.at[kind, 1], recv_sem.at[0, 0, 0], partner).wait_send()

        @pl.when(jnp.logical_not(inner))
        def _():
            remote(ref, own_sem.at[kind, 2], recv_sem.at[0, 0, 0], partner).wait_send()

        @pl.when(inner)
        def _():
            for index in range(2):
                remote(ref, relay_sem.at[kind, index], recv_sem.at[0, 0, 0], partner).wait_send()


def fits(ways, members, conv_weight, w_query, w_out):
    taps, depth, columns = conv_weight.shape
    rows = w_out.shape[0]
    return (
        ways == 8
        and members == 4
        and columns == UNITS * 128
        and depth % 16 == 0
        and rows == HEAD_V
        and HEADS == ways
        and rows % (16 * UNITS) == 0
    )


def encoder_stage(
    tokens, stem_weight, vectors, cosine, sine, conv_weight, w_query, w_key, w_value, w_out
):
    count = tokens.shape[0]
    channels = stem_weight.shape[1]
    taps, depth, columns = conv_weight.shape
    rows = w_out.shape[0]
    ways = lax.axis_size("dp")
    members = lax.axis_size("seq")
    chips = ways // 2
    vmem = pl.BlockSpec(memory_space=pltpu.VMEM)
    hbm = pl.BlockSpec(memory_space=pl.ANY)
    dma = pltpu.SemaphoreType.DMA
    return pl.pallas_call(
        encoder_kernel,
        out_shape=jax.ShapeDtypeStruct((count, columns), jnp.bfloat16),
        in_specs=[vmem] * 8 + [hbm] * 5,
        out_specs=vmem,
        scratch_shapes=[
            pltpu.VMEM((count, columns), jnp.bfloat16),
            pltpu.VMEM((members, count, HEAD_K), jnp.bfloat16),
            pltpu.VMEM((members, count, HEAD_V), jnp.bfloat16),
            pltpu.VMEM((GROUP + 2 * SPAN, count), jnp.float32),
            pltpu.VMEM((POOL_B + 1, count, GROUP), jnp.bfloat16),
            pltpu.VMEM((POOL_A, GROUP, channels), jnp.bfloat16),
            pltpu.VMEM((count, channels), jnp.float32),
            pltpu.VMEM(((POOL_B + 4) * count, channels), jnp.bfloat16),
            pltpu.VMEM((8, GROUP), jnp.int32),
            pltpu.VMEM((8, GROUP), jnp.int32),
            pltpu.VMEM((ways, UNITS, taps, depth, columns // UNITS), jnp.bfloat16),
            pltpu.VMEM((ways, rows, HEADS * HEAD_K + HEAD_K + HEAD_V), jnp.bfloat16),
            pltpu.VMEM((ways, rows, columns), jnp.bfloat16),
            dma((2, members)),
            dma((2, members)),
            dma((2,)),
            dma((2,)),
            dma((3,)),
            dma((3, chips, UNITS)),
            dma((UNITS // 2,)),
            dma((3,)),
            dma((3,)),
            dma((3,)),
            dma((3,)),
            dma((3, 3)),
            dma((3, 2)),
        ],
        compiler_params=pltpu.CompilerParams(
            collective_id=0, has_side_effects=True, vmem_limit_bytes=56 * 2**20
        ),
        name="encoder_stage",
    )(tokens, stem_weight, *vectors, cosine, sine, conv_weight, w_query, w_key, w_value, w_out)


def gather_conv(conv_weight):
    taps, depth, columns = conv_weight.shape
    members = lax.axis_size("seq")
    place = lax.axis_index("seq")
    for row_parts in (2, 1, 3):
        column_parts = members // row_parts
        if members % row_parts or depth % (16 * row_parts) or columns % (256 * column_parts):
            continue
        depth_part = depth // row_parts
        column_part = columns // column_parts
        piece = lax.dynamic_slice(
            conv_weight,
            (0, place // column_parts * depth_part, place % column_parts * column_part),
            (taps, depth_part, column_part),
        )
        full = lax.all_gather(piece, ("dp", "seq"), axis=0, tiled=False)
        return full.reshape(-1, row_parts, column_parts, taps, depth_part, column_part)
    full = lax.all_gather(conv_weight, "dp", axis=0, tiled=False)
    return full[:, None, None]


def gather_rows(weight):
    members = lax.axis_size("seq")
    rows = weight.shape[0] // members
    piece = lax.dynamic_slice_in_dim(weight, lax.axis_index("seq") * rows, rows, axis=0)
    return lax.all_gather(piece, ("dp", "seq"), axis=0, tiled=True)


def body(
    tokens,
    stem_weight,
    stem_bias,
    conv_gain,
    conv_weight,
    conv_bias,
    attn_gain,
    w_query,
    w_key,
    w_value,
    w_out,
):
    seq_local = tokens.shape[1]
    rows_att = seq_local // GROUP
    tokens = tokens.reshape(rows_att, GROUP)
    size = lax.axis_size("seq")
    rows = w_out.shape[0]
    split = HEADS * HEAD_K
    if fits(lax.axis_size("dp"), size, conv_weight, w_query, w_out):
        half_dim = HEAD_K // 2
        freqs = 10000.0 ** (-jnp.arange(half_dim, dtype=jnp.float32) / half_dim)
        positions = lax.axis_index("seq") * rows_att + jnp.arange(rows_att, dtype=jnp.int32)
        angles = positions.astype(jnp.float32)[:, None] * freqs[None, :]
        return encoder_stage(
            tokens,
            stem_weight,
            [vector[None] for vector in (stem_bias, conv_gain, conv_bias, attn_gain)],
            jnp.cos(angles),
            jnp.sin(angles),
            conv_weight,
            w_query,
            w_key,
            w_value,
            w_out,
        )[None]
    else:
        full_conv = gather_conv(conv_weight)
        projections = gather_rows(jnp.concatenate([w_query, w_key, w_value], axis=1))
        first_rows = projections[:, : split + HEAD_K]
        value_rows = projections[:, split + HEAD_K :]
        full_out = gather_rows(w_out)
        forward = [(i, i + 1) for i in range(size - 1)]
        backward = [(i + 1, i) for i in range(size - 1)]
        low = lax.ppermute(tokens[-1:], "seq", forward)
        high = lax.ppermute(tokens[:1], "seq", backward)
        ext = stem_stage(tokens, low, high, stem_weight, stem_bias, conv_gain)
        coarse = conv_stage(ext, full_conv, conv_bias)
    residual = coarse.astype(jnp.float32)
    hidden = rms_scale(residual, attn_gain).astype(jnp.bfloat16)
    projected = jnp.dot(hidden, first_rows, preferred_element_type=jnp.float32)
    query = projected[:, :split]
    keys = projected[:, split:]
    values = jnp.dot(hidden, value_rows, preferred_element_type=jnp.float32)
    half_dim = HEAD_K // 2
    freqs = 10000.0 ** (-jnp.arange(half_dim, dtype=jnp.float32) / half_dim)
    positions = lax.axis_index("seq") * rows_att + jnp.arange(rows_att, dtype=jnp.int32)
    angles = positions.astype(jnp.float32)[:, None] * freqs[None, :]
    query = rotate(query.reshape(rows_att, HEADS, HEAD_K), angles[:, None, :]).astype(jnp.bfloat16)
    keys = rotate(keys, angles).astype(jnp.bfloat16)
    pair = jnp.concatenate([keys, values.astype(jnp.bfloat16)], axis=1)
    pair = lax.all_gather(pair, "seq", axis=0, tiled=True)
    keys_all, values_all = pair[:, :HEAD_K], pair[:, HEAD_K:]
    scores = jnp.einsum(
        "rhd,kd->hrk", query, keys_all, preferred_element_type=jnp.float32
    ) * HEAD_K ** (-0.5)
    weights = jax.nn.softmax(scores, axis=-1).astype(jnp.bfloat16)
    mixed = jnp.einsum(
        "hrk,kd->rhd", weights, values_all, preferred_element_type=jnp.float32
    ).astype(jnp.bfloat16)
    mixed = mixed.reshape(rows_att, HEADS * HEAD_V)
    out = jnp.dot(mixed, full_out, preferred_element_type=jnp.float32)
    return (residual + out).astype(jnp.bfloat16)[None]


def solution(mesh):
    in_specs = (
        P("dp", "seq"),
        P(),
        P(),
        P(),
        P(None, "dp", None),
        P(),
        P(),
        P("dp", None),
        P("dp", None),
        P("dp", None),
        P("dp", None),
    )
    out_specs = P("dp", "seq", None)
    return jax.shard_map(body, mesh=mesh, in_specs=in_specs, out_specs=out_specs, check_vma=False)
```

```python
import functools
import math

import jax
import jax.numpy as jnp
from jax import lax
from jax.experimental import pallas as pl
from jax.experimental.pallas import tpu as pltpu
from jax.sharding import PartitionSpec as P

HEADS = 8
HEAD_K = 128
HEAD_V = 192
KW_STEM = 15
KW = 5
POOL_A = 8
POOL_B = 16
GROUP = POOL_A * POOL_B
SPAN = 24

epsilon = 1e-06


def rms_scale(values, gain):
    return values * lax.rsqrt(jnp.mean(values * values, axis=-1, keepdims=True) + epsilon) * gain


def rotate(values, angles):
    half_dim = values.shape[-1] // 2
    first = values[..., :half_dim]
    second = values[..., half_dim:]
    cosine = jnp.cos(angles)
    sine = jnp.sin(angles)
    return jnp.concatenate(
        [first * cosine - second * sine, second * cosine + first * sine], axis=-1
    )


def stem_kernel(
    tok_ref, low_ref, high_ref, weight_ref, bias_ref, gain_ref, ext_ref, text_ref, hot_ref, shifted_ref, rows_ref
):
    stem_compute(
        tok_ref,
        low_ref[...],
        high_ref[...],
        weight_ref,
        bias_ref,
        gain_ref,
        ext_ref,
        text_ref,
        hot_ref,
        shifted_ref,
        rows_ref,
    )


def stem_shift(weight_ref, shifted_ref):
    source = lax.broadcasted_iota(jnp.int32, (GROUP, weight_ref.shape[0]), 1)
    target = lax.broadcasted_iota(jnp.int32, (GROUP, weight_ref.shape[0]), 0)
    tap = source // 4
    base = source - 4 * tap
    for offset in range(POOL_A):
        pick = (target == base * SPAN + offset + tap + 1).astype(jnp.float32).astype(jnp.bfloat16)
        shifted_ref[offset] = jnp.dot(
            pick, weight_ref[...], preferred_element_type=jnp.float32
        ).astype(jnp.bfloat16)


def hot_of(span):
    planes = [(span == float(code)).astype(jnp.float32) for code in range(1, 5)]
    planes.append(jnp.zeros((GROUP - 4 * SPAN, span.shape[1]), jnp.float32))
    return jnp.concatenate(planes, axis=0).T.astype(jnp.bfloat16)


def stem_inside(tok_ref, text_ref, hot_ref):
    text_ref[SPAN : SPAN + GROUP, :] = tok_ref[...].astype(jnp.float32).T
    for j in range(1, POOL_B - 1):
        hot_ref[j] = hot_of(text_ref[8 * j + SPAN - 8 : 8 * j + 2 * SPAN - 8, :])


def stem_outside(low, high, text_ref, hot_ref):
    count = text_ref.shape[1]
    lane = lax.broadcasted_iota(jnp.int32, (SPAN, count), 1)
    before = low.astype(jnp.float32)
    after = high.astype(jnp.float32)
    text_ref[0:SPAN, :] = jnp.where(
        lane == 0, before[GROUP - SPAN :, :], pltpu.roll(text_ref[GROUP : GROUP + SPAN, :], 1, 1)
    )
    text_ref[SPAN + GROUP :, :] = jnp.where(
        lane == count - 1, after[:SPAN, :], pltpu.roll(text_ref[SPAN : 2 * SPAN, :], count - 1, 1)
    )
    for j in (0, POOL_B - 1):
        hot_ref[j] = hot_of(text_ref[8 * j + SPAN - 8 : 8 * j + 2 * SPAN - 8, :])
    edge = jnp.where(
        lane == 0,
        text_ref[0:SPAN, :],
        jnp.where(
            lane == 1,
            pltpu.roll(text_ref[8 : 8 + SPAN, :], 1, 1),
            jnp.where(
                lane == 2,
                pltpu.roll(text_ref[GROUP + SPAN - 8 : GROUP + 2 * SPAN - 8, :], 3, 1),
                pltpu.roll(text_ref[GROUP + SPAN : GROUP + 2 * SPAN, :], 4, 1),
            ),
        ),
    )
    hot_ref[POOL_B] = hot_of(edge)


def column_of(row, count):
    return jnp.broadcast_to(row.astype(jnp.float32), (8, count)).T[:, 0:1]


def stem_block(j, bias_ref, gain_ref, ext_ref, hot_ref, shifted_ref, rows_ref):
    count, channels = rows_ref.shape
    width = 256
    hot = hot_ref[j]
    for chunk in range(channels // width):
        columns = slice(chunk * width, (chunk + 1) * width)
        best = None
        for offset in range(POOL_A):
            stem = jnp.dot(hot, shifted_ref[offset, :, columns], preferred_element_type=jnp.float32)
            best = stem if best is None else jnp.maximum(best, stem)
        pooled = jax.nn.gelu(best + bias_ref[columns].reshape(1, width)).astype(jnp.bfloat16)
        rows_ref[:, columns] = pooled.astype(jnp.float32)
    pooled = rows_ref[...]
    start = pl.multiple_of((j + 2) * count, count)
    ext_ref[pl.ds(start, count), :] = rms_scale(pooled, gain_ref[...].reshape(1, channels)).astype(jnp.bfloat16)


def stem_edges(place, last_place, ext_ref, rows_ref):
    count, channels = rows_ref.shape
    edges = ext_ref[(POOL_B + 2) * count : (POOL_B + 3) * count, :].astype(jnp.float32)
    left_keep = (place > 0).astype(jnp.float32)
    right_keep = (place < last_place).astype(jnp.float32)
    spot = lax.broadcasted_iota(jnp.int32, (count, channels), 0)
    for index in range(2):
        inner = ext_ref[(POOL_B + index) * count : (POOL_B + index + 1) * count, :]
        moved = pltpu.roll(inner.astype(jnp.float32), 1, 0)
        ext_ref[index * count : (index + 1) * count, :] = jnp.where(
            spot == 0, edges[index : index + 1, :] * left_keep, moved
        ).astype(jnp.bfloat16)
        inner = ext_ref[(2 + index) * count : (3 + index) * count, :]
        moved = pltpu.roll(inner.astype(jnp.float32), count - 1, 0)
        at = POOL_B + 2 + index
        ext_ref[at * count : (at + 1) * count, :] = jnp.where(
            spot == count - 1, edges[2 + index : 3 + index, :] * right_keep, moved
        ).astype(jnp.bfloat16)


def stem_compute(
    tok_ref, low, high, weight_ref, bias_ref, gain_ref, ext_ref, text_ref, hot_ref, shifted_ref, rows_ref
):
    stem_shift(weight_ref, shifted_ref)
    stem_inside(tok_ref, text_ref, hot_ref)
    stem_outside(column_of(low, GROUP), column_of(high, GROUP), text_ref, hot_ref)

    def block(j, carry):
        stem_block(j, bias_ref, gain_ref, ext_ref, hot_ref, shifted_ref, rows_ref)
        return carry

    lax.fori_loop(0, POOL_B + 1, block, 0)
    stem_edges(lax.axis_index("seq"), lax.axis_size("seq") - 1, ext_ref, rows_ref)


def stem_stage(tokens, low, high, stem_weight, stem_bias, conv_gain):
    count = tokens.shape[0]
    channels = stem_weight.shape[1]
    return pl.pallas_call(
        stem_kernel,
        out_shape=jax.ShapeDtypeStruct(((POOL_B + 4) * count, channels), jnp.bfloat16),
        in_specs=[pl.BlockSpec(memory_space=pltpu.VMEM)] * 6,
        out_specs=pl.BlockSpec(memory_space=pltpu.VMEM),
        scratch_shapes=[
            pltpu.VMEM((GROUP + 2 * SPAN, count), jnp.float32),
            pltpu.VMEM((POOL_B + 1, count, GROUP), jnp.bfloat16),
            pltpu.VMEM((POOL_A, GROUP, channels), jnp.bfloat16),
            pltpu.VMEM((count, channels), jnp.float32),
        ],
        cost_estimate=pl.CostEstimate(
            flops=20_000_000_000, bytes_accessed=4_000_000, transcendentals=1_600_000
        ),
        name="stem_stage",
    )(tokens, low, high, stem_weight, stem_bias, conv_gain)


def conv_kernel(count, ext_ref, weight_ref, bias_ref, coarse_ref):
    group = 4
    width = weight_ref.shape[-1]
    channels = ext_ref.shape[1]

    def block(m, carry):
        most, least = carry
        total = None
        for tap in range(KW):
            start = pl.multiple_of((m * group + tap) * count, count)
            part = jnp.dot(
                ext_ref[pl.ds(start, group * count), :],
                weight_ref[:, :, 0, tap].reshape(channels, width),
                preferred_element_type=jnp.float32,
            )
            total = part if total is None else total + part
        for index in range(group):
            piece = total[index * count : (index + 1) * count]
            most = jnp.maximum(most, piece)
            least = jnp.minimum(least, piece)
        return most, least

    big = jnp.full((count, width), jnp.finfo(jnp.float32).max, jnp.float32)
    most, least = lax.fori_loop(0, POOL_B // group, block, (-big, big))
    bias = bias_ref[...]
    coarse_ref[...] = jnp.maximum(jax.nn.gelu(most + bias), jax.nn.gelu(least + bias)).astype(
        jnp.bfloat16
    )


def conv_stage(ext, weight, conv_bias):
    count = ext.shape[0] // (POOL_B + 4)
    ways, row_parts, column_parts, taps, depth, columns = weight.shape
    width = 256
    steps = columns // width
    return pl.pallas_call(
        functools.partial(conv_kernel, count),
        grid=(column_parts, steps),
        out_shape=jax.ShapeDtypeStruct((count, column_parts * columns), jnp.bfloat16),
        in_specs=[
            pl.BlockSpec(ext.shape, lambda b, n: (0, 0), pipeline_mode=pl.Buffered(1)),
            pl.BlockSpec(
                (ways, row_parts, 1, taps, depth, width), lambda b, n: (0, 0, b, 0, 0, n)
            ),
            pl.BlockSpec((1, width), lambda b, n: (0, b * steps + n)),
        ],
        out_specs=pl.BlockSpec((count, width), lambda b, n: (0, b * steps + n)),
        cost_estimate=pl.CostEstimate(
            flops=24_000_000_000, bytes_accessed=16_000_000, transcendentals=400_000
        ),
        name="conv_stage",
    )(ext, weight, conv_bias[None])


MESH = pl.DeviceIdType.MESH


UNITS = 12
GROUPS = 3


def encoder_kernel(
    tok_ref,
    stem_weight_ref,
    stem_bias_ref,
    gain_ref,
    conv_bias_ref,
    attn_gain_ref,
    conv_ref,
    query_ref,
    keyw_ref,
    valuew_ref,
    outw_ref,
    out_ref,
    coarse_ref,
    key_ref,
    value_ref,
    text_ref,
    hot_ref,
    shifted_ref,
    rows_ref,
    turn_ref,
    ext_ref,
    low_ref,
    high_ref,
    conv_full,
    proj_full,
    outw_full,
    pair_send,
    pair_recv,
    halo_send,
    halo_recv,
    local_sem,
    recv_sem,
    partner_sem,
    x_sem,
    y_sem,
    partner_send,
    own_sem,
    relay_sem,
):
    wide = out_ref.shape[1]
    members = lax.axis_size("seq")
    me = lax.axis_index("dp")
    place = lax.axis_index("seq")
    chip = me // 2
    core = me % 2
    chips = lax.axis_size("dp") // 2
    partner = (chip * 2 + 1 - core, place)
    count = tok_ref.shape[0]
    depth, width = conv_full.shape[5:]
    unit_rows = proj_full.shape[1] // UNITS
    kinds = GROUPS + 2
    split = HEADS * HEAD_K
    middle = split + HEAD_K

    along_x = place + 1 - 2 * (place % 2)
    along_y = place + 2 - 4 * (place // 2)
    across = 3 - place
    mine = (place % 2 + place // 2) % 2
    theirs = 1 - mine
    x_target = (me, along_x)
    y_target = (me, along_y)

    sources = (1 + chip % 2, (chip + 2) % chips, 3 - 3 * (chip % 2))
    inner = (chip > 0) & (chip < chips - 1)
    relays = (3 * (chip - 1), None, chips - 1 - chip)

    first = (place, 4 + mine)
    x_out = ((0, place, None), (1, along_y, 1), (2, 4 + mine, 0))
    y_out = ((0, place, None), (1, along_x, 0), (2, 4 + mine, 1))
    x_in = ((0, along_x, None), (1, across, 1), (2, 4 + theirs, 0))
    y_in = ((0, along_y, None), (1, across, 0), (2, 4 + theirs, 1))

    def full_of(kind):
        return (*(conv_full.at[group] for group in range(GROUPS)), proj_full, outw_full)[kind]

    def part(kind, way, pair, half=None):
        full = full_of(kind).at[way]
        if kind < GROUPS:
            return full.at[pair] if half is None else full.at[pair, half]
        unit = 2 * pair + (half or 0)
        span = 2 if half is None else 1
        return full.at[pl.ds(pl.multiple_of(unit * unit_rows, unit_rows), span * unit_rows)]

    def remote(ref, send_sem, recv, target):
        return pltpu.make_async_remote_copy(ref, ref, send_sem, recv, target, MESH)

    def arrived(ref, recv):
        remote(ref, x_sem.at[0], recv, partner).wait_recv()

    def to_partner(kind, ref):
        remote(ref, partner_send.at[kind], partner_sem.at[kind], partner).start()

    def own(kind, i):
        ref = part(kind, me, first[i])
        recv = recv_sem.at[kind, chip, i]

        @pl.when(chip < chips - 1)
        def _():
            remote(ref, own_sem.at[kind, 0], recv, (me + 2, place)).start()

        @pl.when(chip > 0)
        def _():
            remote(ref, own_sem.at[kind, 1], recv, (me - 2, place)).start()

        @pl.when(jnp.logical_not(inner))
        def _():
            far = 2 * (chips - 1 - chip) + core
            remote(ref, own_sem.at[kind, 2], recv, (far, place)).start()

    def plane_send(kind, origin, k):
        way = 2 * origin + core
        for base, out, sem, target in ((2, x_out, x_sem, x_target), (5, y_out, y_sem, y_target)):
            k, pair, half = out[k]
            recv = recv_sem.at[kind, origin, base + k]
            remote(part(kind, way, pair, half), sem.at[kind], recv, target).start()

    def z_step(kind, i, j):
        origin = sources[j]
        ref = part(kind, 2 * origin + core, first[i])
        recv = recv_sem.at[kind, origin, i]
        arrived(ref, recv)
        if relays[j] is not None:

            @pl.when(inner)
            def _():
                remote(ref, relay_sem.at[kind, j // 2], recv, (2 * relays[j] + core, place)).start()

        plane_send(kind, origin, 2 * i)
        to_partner(kind, ref)

    def plane_step(kind, i, j):
        origin = sources[j]
        way = 2 * origin + core
        for ks in ((0,), (1, 2))[i : i + 1]:
            for k in ks:
                for base, into in ((2, x_in), (5, y_in)):
                    _, pair, half = into[k]
                    ref = part(kind, way, pair, half)
                    arrived(ref, recv_sem.at[kind, origin, base + k])
                    to_partner(kind, ref)
        if i == 0:
            plane_send(kind, origin, 1)

    stream = [(kind, i) for kind in range(kinds) for i in range(2)]
    events = []
    for turn in range(len(stream) + 1):
        for j in range(3):
            at = turn - (j == 1)
            if 0 <= at < len(stream) and not (turn == len(stream) and j != 1):
                events.append((at, j))
    def event(n):
        if n < 100:
            at, j = events[n]
            z_step(*stream[at], j)
            if at == 1 and j == 0:
                own(*stream[2])
            if at > 0 and j == 2 and at + 2 < len(stream):
                own(*stream[at + 2])
        else:
            at, j = events[n - 100]
            plane_step(*stream[at], j)

    def run(*some):
        for n in some:
            event(n)

    def plane(*some):
        return [100 + n for n in some]

    def event_of(number, lists):
        for index, some in enumerate(lists):

            @pl.when(number == index)
            def _():
                run(*some)

    def local_copies(kind):
        if kind < GROUPS:
            for pair in range(UNITS // 2):
                for half in range(2):
                    rows = pl.ds(pair * depth, depth)
                    columns = pl.ds((2 * kind + half) * width, width)
                    yield conv_ref.at[:, rows, columns], part(kind, me, pair, half)
        elif kind == GROUPS:
            yield query_ref, proj_full.at[me, :, pl.ds(0, split)]
            yield keyw_ref, proj_full.at[me, :, pl.ds(split, HEAD_K)]
            yield valuew_ref, proj_full.at[me, :, pl.ds(middle, HEAD_V)]
        else:
            yield outw_ref, outw_full.at[me]

    def local_start(kind):
        for a, b in local_copies(kind):
            pltpu.make_async_copy(a, b, local_sem.at[kind]).start()

    def local_wait(kind):
        whole = full_of(kind).at[me]
        pltpu.make_async_copy(whole, whole, local_sem.at[kind]).wait()

    def own_partner(kind):
        to_partner(kind, full_of(kind).at[me])

    barrier = pltpu.get_barrier_semaphore()
    pl.semaphore_signal(barrier, inc=1, device_id=partner, device_id_type=MESH)
    for turn in (1, chips - 1):
        neighbour = (chip + turn) % chips * 2 + core
        pl.semaphore_signal(barrier, inc=1, device_id=(neighbour, place), device_id_type=MESH)
    for turn in range(1, members):
        pl.semaphore_signal(
            barrier, inc=1, device_id=(me, (place + turn) % members), device_id_type=MESH
        )
    local_start(0)
    local_wait(0)
    pl.semaphore_wait(barrier, members + 2)

    own(0, 0)
    right = (place + 1) % members
    left = (place + members - 1) % members
    halo = [
        pltpu.make_async_remote_copy(
            tok_ref.at[count - 8 : count], low_ref, halo_send.at[0], halo_recv.at[0], (me, right), MESH
        ),
        pltpu.make_async_remote_copy(
            tok_ref.at[0:8], high_ref, halo_send.at[1], halo_recv.at[1], (me, left), MESH
        ),
    ]
    for copy in halo:
        copy.start()
    stem_shift(stem_weight_ref, shifted_ref)
    own(0, 1)
    own_partner(0)
    for kind in range(1, kinds):
        local_start(kind)
    stem_inside(tok_ref, text_ref, hot_ref)

    half_dim = HEAD_K // 2
    lane = lax.broadcasted_iota(jnp.int32, (count, HEAD_K), 1)
    step = lane % half_dim
    freqs = jnp.exp(step.astype(jnp.float32) * (-math.log(10000.0) / half_dim))
    position = place * count + lax.broadcasted_iota(jnp.int32, (count, HEAD_K), 0)
    angles = position.astype(jnp.float32) * freqs
    turn_ref[0] = jnp.cos(angles)
    sine = jnp.sin(angles)
    turn_ref[1] = jnp.where(lane < half_dim, -sine, sine)

    def outside():
        for copy in halo:
            copy.wait()
        low = jnp.where(place > 0, low_ref[7:8], 0)
        high = jnp.where(place < members - 1, high_ref[0:1], 0)
        stem_outside(column_of(low, GROUP), column_of(high, GROUP), text_ref, hot_ref)
        for kind in range(1, kinds):
            local_wait(kind)
            own_partner(kind)

    early_events = [[n, *plane(*range(max(n - 2, 0), n - 1))] for n in range(7)]
    early_events += [[7, *plane(5), 8, *plane(6)], []]

    def stem_round(r, nothing):
        def block(step, nothing):
            j = (step + 1) % (POOL_B + 1)
            stem_block(j, stem_bias_ref, gain_ref, ext_ref, hot_ref, shifted_ref, rows_ref)
            return nothing

        lax.fori_loop(2 * r, 2 * r + 2 - r // 8, block, 0)
        pl.when(r == 0)(outside)
        event_of(r, early_events)
        return nothing

    lax.fori_loop(0, POOL_B // 2 + 1, stem_round, 0)
    stem_edges(place, members - 1, ext_ref, rows_ref)

    group = 8
    channels = ext_ref.shape[1]
    big = jnp.full((count, width), jnp.finfo(jnp.float32).max, jnp.float32)

    def conv_panel(turn, half, after):
        weight_ref = conv_full.at[turn, :, :, half]

        def block(m, carry):
            most, least = carry
            weight = jnp.concatenate(
                [weight_ref[:, :, tap].reshape(channels, width) for tap in range(KW)], axis=0
            )
            rows = jnp.concatenate(
                [
                    ext_ref[pl.ds(pl.multiple_of((m * group + tap) * count, count), group * count), :]
                    for tap in range(KW)
                ],
                axis=1,
            )
            total = jnp.dot(rows, weight, preferred_element_type=jnp.float32)
            for index in range(group):
                piece = total[index * count : (index + 1) * count]
                most = jnp.maximum(most, piece)
                least = jnp.minimum(least, piece)
            after(m)
            return most, least

        most, least = lax.fori_loop(0, POOL_B // group, block, (-big, big))
        at = pl.multiple_of((2 * turn + half) * width, width)
        bias = conv_bias_ref[pl.ds(at, width)].reshape(1, width)
        coarse_ref[:, pl.ds(at, width)] = jnp.maximum(
            jax.nn.gelu(most + bias), jax.nn.gelu(least + bias)
        ).astype(jnp.bfloat16)

    late_events = [
        [10, 11, *plane(8)],
        [12, 13, *plane(9)],
        [14, *plane(10, 11)],
        [15, *plane(12)],
        [17, 18, *plane(14)],
        [19, *plane(15, 16)],
        [20, 21, *plane(17)],
        [22, *plane(18)],
        [24, *plane(20, 21)],
        [25, 26, *plane(22)],
        [27, *plane(23, 24)],
        [28, *plane(25, 26)],
    ]
    between = [[9, *plane(7)], [16, *plane(13)], [23, *plane(19)]]

    def conv_turn(t, nothing):
        for turn in range(GROUPS):

            @pl.when(t == 2 * turn)
            def _():
                run(*between[turn])
                arrived(conv_full.at[turn, pl.ds(0, chips)], partner_sem.at[turn])

        conv_panel(t // 2, t % 2, lambda m: event_of(POOL_B // group * t + m, late_events))
        return nothing

    lax.fori_loop(0, 2 * GROUPS, conv_turn, 0)
    arrived(proj_full.at[pl.ds(0, chips)], partner_sem.at[GROUPS])

    def weight(begin, end):
        return proj_full[:, :, begin:end].reshape(wide, end - begin)

    def turned(head):
        return (head * turn_ref[0] + pltpu.roll(head, HEAD_K // 2, 1) * turn_ref[1]).astype(jnp.bfloat16)

    hidden = rms_scale(coarse_ref[...].astype(jnp.float32), attn_gain_ref[...].reshape(1, -1)).astype(
        jnp.bfloat16
    )
    key_ref[place] = turned(
        jnp.dot(hidden, weight(split, middle), preferred_element_type=jnp.float32)
    )
    value_ref[place] = jnp.dot(
        hidden, weight(middle, middle + HEAD_V), preferred_element_type=jnp.float32
    ).astype(jnp.bfloat16)
    pairs = []
    for turn in range(1, members):
        for index, ref in enumerate((key_ref, value_ref)):
            copy = pltpu.make_async_remote_copy(
                ref.at[place],
                ref.at[place],
                pair_send.at[index, turn],
                pair_recv.at[index, place],
                (me, (place + turn) % members),
                MESH,
            )
            copy.start()
            pairs.append(copy)
    query = jnp.dot(hidden, weight(0, split), preferred_element_type=jnp.float32)
    run(29, *plane(27))
    for turn in range(1, members):
        spot = (place + turn) % members
        for index, ref in enumerate((key_ref, value_ref)):
            arrived(ref.at[spot], pair_recv.at[index, spot])
    keys = key_ref[...].reshape(members * count, HEAD_K)
    values = value_ref[...].reshape(members * count, HEAD_V)
    mixes = []
    for head in range(HEADS):
        scores = lax.dot_general(
            turned(query[:, head * HEAD_K : (head + 1) * HEAD_K]),
            keys,
            (((1,), (1,)), ((), ())),
            preferred_element_type=jnp.float32,
        ) * HEAD_K ** (-0.5)
        raised = jnp.exp(scores - jnp.max(scores, axis=-1, keepdims=True))
        weights = (raised / jnp.sum(raised, axis=-1, keepdims=True)).astype(jnp.bfloat16)
        mixes.append(
            jnp.dot(weights, values, preferred_element_type=jnp.float32).astype(jnp.bfloat16)
        )
        if head == 3:
            run(*plane(28))
    run(*plane(29))
    arrived(outw_full.at[pl.ds(0, chips)], partner_sem.at[GROUPS + 1])
    total = coarse_ref[...].astype(jnp.float32)
    for head in range(HEADS):
        total = total + jnp.dot(mixes[head], outw_full[head], preferred_element_type=jnp.float32)
    out_ref[...] = total.astype(jnp.bfloat16)
    for copy in pairs:
        copy.wait_send()
    for kind in range(kinds):
        whole = full_of(kind).at[0]
        remote(whole, x_sem.at[kind], recv_sem.at[0, 0, 0], x_target).wait_send()
        remote(whole, y_sem.at[kind], recv_sem.at[0, 0, 0], y_target).wait_send()
        every = full_of(kind).at[pl.ds(0, chips)]
        remote(every, partner_send.at[kind], recv_sem.at[0, 0, 0], partner).wait_send()
        ref = full_of(kind).at[0, pl.ds(0, 2 if kind < GROUPS else 4 * unit_rows)]

        @pl.when(chip < chips - 1)
        def _():
            remote(ref, own_sem.at[kind, 0], recv_sem.at[0, 0, 0], partner).wait_send()

        @pl.when(chip > 0)
        def _():
            remote(ref, own_sem.at[kind, 1], recv_sem.at[0, 0, 0], partner).wait_send()

        @pl.when(jnp.logical_not(inner))
        def _():
            remote(ref, own_sem.at[kind, 2], recv_sem.at[0, 0, 0], partner).wait_send()

        @pl.when(inner)
        def _():
            for index in range(2):
                remote(ref, relay_sem.at[kind, index], recv_sem.at[0, 0, 0], partner).wait_send()


def fits(ways, members, conv_weight, w_query, w_out):
    taps, depth, columns = conv_weight.shape
    rows = w_out.shape[0]
    return (
        ways == 8
        and members == 4
        and columns == 2 * GROUPS * 256
        and depth == UNITS // 2 * 16
        and rows == HEAD_V
        and HEADS == ways
        and rows % (16 * UNITS) == 0
    )


def encoder_stage(
    tokens, stem_weight, vectors, conv_weight, w_query, w_key, w_value, w_out
):
    count = tokens.shape[0]
    channels = stem_weight.shape[1]
    taps, depth, columns = conv_weight.shape
    rows = w_out.shape[0]
    ways = lax.axis_size("dp")
    members = lax.axis_size("seq")
    chips = ways // 2
    vmem = pl.BlockSpec(memory_space=pltpu.VMEM)
    hbm = pl.BlockSpec(memory_space=pl.ANY)
    dma = pltpu.SemaphoreType.DMA
    kinds = GROUPS + 2
    return pl.pallas_call(
        encoder_kernel,
        out_shape=jax.ShapeDtypeStruct((count, columns), jnp.bfloat16),
        in_specs=[vmem] * 6 + [hbm] * 5,
        out_specs=vmem,
        scratch_shapes=[
            pltpu.VMEM((count, columns), jnp.bfloat16),
            pltpu.VMEM((members, count, HEAD_K), jnp.bfloat16),
            pltpu.VMEM((members, count, HEAD_V), jnp.bfloat16),
            pltpu.VMEM((GROUP + 2 * SPAN, count), jnp.float32),
            pltpu.VMEM((POOL_B + 1, count, GROUP), jnp.bfloat16),
            pltpu.VMEM((POOL_A, GROUP, channels), jnp.bfloat16),
            pltpu.VMEM((count, channels), jnp.float32),
            pltpu.VMEM((2, count, HEAD_K), jnp.float32),
            pltpu.VMEM(((POOL_B + 4) * count, channels), jnp.bfloat16),
            pltpu.VMEM((8, GROUP), jnp.int32),
            pltpu.VMEM((8, GROUP), jnp.int32),
            pltpu.VMEM(
                (GROUPS, ways, UNITS // 2, 2, taps, depth // 6, columns // (2 * GROUPS)), jnp.bfloat16
            ),
            pltpu.VMEM((ways, rows, HEADS * HEAD_K + HEAD_K + HEAD_V), jnp.bfloat16),
            pltpu.VMEM((ways, rows, columns), jnp.bfloat16),
            dma((2, members)),
            dma((2, members)),
            dma((2,)),
            dma((2,)),
            dma((kinds,)),
            dma((kinds, chips, 8)),
            dma((kinds,)),
            dma((kinds,)),
            dma((kinds,)),
            dma((kinds,)),
            dma((kinds, 3)),
            dma((kinds, 2)),
        ],
        compiler_params=pltpu.CompilerParams(
            collective_id=0, has_side_effects=True, vmem_limit_bytes=56 * 2**20
        ),
        name="encoder_stage",
    )(tokens, stem_weight, *vectors, conv_weight, w_query, w_key, w_value, w_out)


def gather_conv(conv_weight):
    taps, depth, columns = conv_weight.shape
    members = lax.axis_size("seq")
    place = lax.axis_index("seq")
    for row_parts in (2, 1, 3):
        column_parts = members // row_parts
        if members % row_parts or depth % (16 * row_parts) or columns % (256 * column_parts):
            continue
        depth_part = depth // row_parts
        column_part = columns // column_parts
        piece = lax.dynamic_slice(
            conv_weight,
            (0, place // column_parts * depth_part, place % column_parts * column_part),
            (taps, depth_part, column_part),
        )
        full = lax.all_gather(piece, ("dp", "seq"), axis=0, tiled=False)
        return full.reshape(-1, row_parts, column_parts, taps, depth_part, column_part)
    full = lax.all_gather(conv_weight, "dp", axis=0, tiled=False)
    return full[:, None, None]


def gather_rows(weight):
    members = lax.axis_size("seq")
    rows = weight.shape[0] // members
    piece = lax.dynamic_slice_in_dim(weight, lax.axis_index("seq") * rows, rows, axis=0)
    return lax.all_gather(piece, ("dp", "seq"), axis=0, tiled=True)


def body(
    tokens,
    stem_weight,
    stem_bias,
    conv_gain,
    conv_weight,
    conv_bias,
    attn_gain,
    w_query,
    w_key,
    w_value,
    w_out,
):
    seq_local = tokens.shape[1]
    rows_att = seq_local // GROUP
    tokens = tokens.reshape(rows_att, GROUP)
    size = lax.axis_size("seq")
    rows = w_out.shape[0]
    split = HEADS * HEAD_K
    if fits(lax.axis_size("dp"), size, conv_weight, w_query, w_out):
        return encoder_stage(
            tokens,
            stem_weight,
            [stem_bias, conv_gain, conv_bias, attn_gain],
            conv_weight,
            w_query,
            w_key,
            w_value,
            w_out,
        )[None]
    else:
        full_conv = gather_conv(conv_weight)
        projections = gather_rows(jnp.concatenate([w_query, w_key, w_value], axis=1))
        first_rows = projections[:, : split + HEAD_K]
        value_rows = projections[:, split + HEAD_K :]
        full_out = gather_rows(w_out)
        forward = [(i, i + 1) for i in range(size - 1)]
        backward = [(i + 1, i) for i in range(size - 1)]
        low = lax.ppermute(tokens[-1:], "seq", forward)
        high = lax.ppermute(tokens[:1], "seq", backward)
        ext = stem_stage(tokens, low, high, stem_weight, stem_bias, conv_gain)
        coarse = conv_stage(ext, full_conv, conv_bias)
    residual = coarse.astype(jnp.float32)
    hidden = rms_scale(residual, attn_gain).astype(jnp.bfloat16)
    projected = jnp.dot(hidden, first_rows, preferred_element_type=jnp.float32)
    query = projected[:, :split]
    keys = projected[:, split:]
    values = jnp.dot(hidden, value_rows, preferred_element_type=jnp.float32)
    half_dim = HEAD_K // 2
    freqs = 10000.0 ** (-jnp.arange(half_dim, dtype=jnp.float32) / half_dim)
    positions = lax.axis_index("seq") * rows_att + jnp.arange(rows_att, dtype=jnp.int32)
    angles = positions.astype(jnp.float32)[:, None] * freqs[None, :]
    query = rotate(query.reshape(rows_att, HEADS, HEAD_K), angles[:, None, :]).astype(jnp.bfloat16)
    keys = rotate(keys, angles).astype(jnp.bfloat16)
    pair = jnp.concatenate([keys, values.astype(jnp.bfloat16)], axis=1)
    pair = lax.all_gather(pair, "seq", axis=0, tiled=True)
    keys_all, values_all = pair[:, :HEAD_K], pair[:, HEAD_K:]
    scores = jnp.einsum(
        "rhd,kd->hrk", query, keys_all, preferred_element_type=jnp.float32
    ) * HEAD_K ** (-0.5)
    weights = jax.nn.softmax(scores, axis=-1).astype(jnp.bfloat16)
    mixed = jnp.einsum(
        "hrk,kd->rhd", weights, values_all, preferred_element_type=jnp.float32
    ).astype(jnp.bfloat16)
    mixed = mixed.reshape(rows_att, HEADS * HEAD_V)
    out = jnp.dot(mixed, full_out, preferred_element_type=jnp.float32)
    return (residual + out).astype(jnp.bfloat16)[None]


def solution(mesh):
    in_specs = (
        P("dp", "seq"),
        P(),
        P(),
        P(),
        P(None, "dp", None),
        P(),
        P(),
        P("dp", None),
        P("dp", None),
        P("dp", None),
        P("dp", None),
    )
    out_specs = P("dp", "seq", None)
    return jax.shard_map(body, mesh=mesh, in_specs=in_specs, out_specs=out_specs, check_vma=False)
```

```python
import functools
import math

import jax
import jax.numpy as jnp
from jax import lax
from jax.experimental import pallas as pl
from jax.experimental.pallas import tpu as pltpu
from jax.sharding import PartitionSpec as P

HEADS = 8
HEAD_K = 128
HEAD_V = 192
KW_STEM = 15
KW = 5
POOL_A = 8
POOL_B = 16
GROUP = POOL_A * POOL_B
SPAN = 24

epsilon = 1e-06


def rms_scale(values, gain):
    return values * lax.rsqrt(jnp.mean(values * values, axis=-1, keepdims=True) + epsilon) * gain


def rotate(values, angles):
    half_dim = values.shape[-1] // 2
    first = values[..., :half_dim]
    second = values[..., half_dim:]
    cosine = jnp.cos(angles)
    sine = jnp.sin(angles)
    return jnp.concatenate(
        [first * cosine - second * sine, second * cosine + first * sine], axis=-1
    )


def stem_kernel(
    tok_ref, low_ref, high_ref, weight_ref, bias_ref, gain_ref, ext_ref, text_ref, hot_ref, shifted_ref, rows_ref
):
    stem_compute(
        tok_ref,
        low_ref[...],
        high_ref[...],
        weight_ref,
        bias_ref,
        gain_ref,
        ext_ref,
        text_ref,
        hot_ref,
        shifted_ref,
        rows_ref,
    )


def stem_shift(weight_ref, shifted_ref):
    source = lax.broadcasted_iota(jnp.int32, (GROUP, weight_ref.shape[0]), 1)
    target = lax.broadcasted_iota(jnp.int32, (GROUP, weight_ref.shape[0]), 0)
    tap = source // 4
    base = source - 4 * tap
    for offset in range(POOL_A):
        pick = (target == base * SPAN + offset + tap + 1).astype(jnp.float32).astype(jnp.bfloat16)
        shifted_ref[offset] = jnp.dot(
            pick, weight_ref[...], preferred_element_type=jnp.float32
        ).astype(jnp.bfloat16)


def hot_of(span):
    planes = [(span == float(code)).astype(jnp.float32) for code in range(1, 5)]
    planes.append(jnp.zeros((GROUP - 4 * SPAN, span.shape[1]), jnp.float32))
    return jnp.concatenate(planes, axis=0).T.astype(jnp.bfloat16)


def stem_inside(tok_ref, text_ref, hot_ref):
    text_ref[SPAN : SPAN + GROUP, :] = tok_ref[...].astype(jnp.float32).T
    for j in range(1, POOL_B - 1):
        hot_ref[j] = hot_of(text_ref[8 * j + SPAN - 8 : 8 * j + 2 * SPAN - 8, :])


def stem_outside(low, high, text_ref, hot_ref):
    count = text_ref.shape[1]
    lane = lax.broadcasted_iota(jnp.int32, (SPAN, count), 1)
    before = low.astype(jnp.float32)
    after = high.astype(jnp.float32)
    text_ref[0:SPAN, :] = jnp.where(
        lane == 0, before[GROUP - SPAN :, :], pltpu.roll(text_ref[GROUP : GROUP + SPAN, :], 1, 1)
    )
    text_ref[SPAN + GROUP :, :] = jnp.where(
        lane == count - 1, after[:SPAN, :], pltpu.roll(text_ref[SPAN : 2 * SPAN, :], count - 1, 1)
    )
    for j in (0, POOL_B - 1):
        hot_ref[j] = hot_of(text_ref[8 * j + SPAN - 8 : 8 * j + 2 * SPAN - 8, :])
    edge = jnp.where(
        lane == 0,
        text_ref[0:SPAN, :],
        jnp.where(
            lane == 1,
            pltpu.roll(text_ref[8 : 8 + SPAN, :], 1, 1),
            jnp.where(
                lane == 2,
                pltpu.roll(text_ref[GROUP + SPAN - 8 : GROUP + 2 * SPAN - 8, :], 3, 1),
                pltpu.roll(text_ref[GROUP + SPAN : GROUP + 2 * SPAN, :], 4, 1),
            ),
        ),
    )
    hot_ref[POOL_B] = hot_of(edge)


def column_of(row, count):
    return jnp.broadcast_to(row.astype(jnp.float32), (8, count)).T[:, 0:1]


def stem_block(j, bias_ref, gain_ref, ext_ref, hot_ref, shifted_ref, rows_ref):
    count, channels = rows_ref.shape
    width = 256
    hot = hot_ref[j]
    for chunk in range(channels // width):
        columns = slice(chunk * width, (chunk + 1) * width)
        best = None
        for offset in range(POOL_A):
            stem = jnp.dot(hot, shifted_ref[offset, :, columns], preferred_element_type=jnp.float32)
            best = stem if best is None else jnp.maximum(best, stem)
        pooled = jax.nn.gelu(best + bias_ref[columns].reshape(1, width)).astype(jnp.bfloat16)
        rows_ref[:, columns] = pooled.astype(jnp.float32)
    pooled = rows_ref[...]
    start = pl.multiple_of((j + 2) * count, count)
    ext_ref[pl.ds(start, count), :] = rms_scale(pooled, gain_ref[...].reshape(1, channels)).astype(jnp.bfloat16)


def stem_edges(place, last_place, ext_ref, rows_ref):
    count, channels = rows_ref.shape
    edges = ext_ref[(POOL_B + 2) * count : (POOL_B + 3) * count, :].astype(jnp.float32)
    left_keep = (place > 0).astype(jnp.float32)
    right_keep = (place < last_place).astype(jnp.float32)
    spot = lax.broadcasted_iota(jnp.int32, (count, channels), 0)
    for index in range(2):
        inner = ext_ref[(POOL_B + index) * count : (POOL_B + index + 1) * count, :]
        moved = pltpu.roll(inner.astype(jnp.float32), 1, 0)
        ext_ref[index * count : (index + 1) * count, :] = jnp.where(
            spot == 0, edges[index : index + 1, :] * left_keep, moved
        ).astype(jnp.bfloat16)
        inner = ext_ref[(2 + index) * count : (3 + index) * count, :]
        moved = pltpu.roll(inner.astype(jnp.float32), count - 1, 0)
        at = POOL_B + 2 + index
        ext_ref[at * count : (at + 1) * count, :] = jnp.where(
            spot == count - 1, edges[2 + index : 3 + index, :] * right_keep, moved
        ).astype(jnp.bfloat16)


def stem_compute(
    tok_ref, low, high, weight_ref, bias_ref, gain_ref, ext_ref, text_ref, hot_ref, shifted_ref, rows_ref
):
    stem_shift(weight_ref, shifted_ref)
    stem_inside(tok_ref, text_ref, hot_ref)
    stem_outside(column_of(low, GROUP), column_of(high, GROUP), text_ref, hot_ref)

    def block(j, carry):
        stem_block(j, bias_ref, gain_ref, ext_ref, hot_ref, shifted_ref, rows_ref)
        return carry

    lax.fori_loop(0, POOL_B + 1, block, 0)
    stem_edges(lax.axis_index("seq"), lax.axis_size("seq") - 1, ext_ref, rows_ref)


def stem_stage(tokens, low, high, stem_weight, stem_bias, conv_gain):
    count = tokens.shape[0]
    channels = stem_weight.shape[1]
    return pl.pallas_call(
        stem_kernel,
        out_shape=jax.ShapeDtypeStruct(((POOL_B + 4) * count, channels), jnp.bfloat16),
        in_specs=[pl.BlockSpec(memory_space=pltpu.VMEM)] * 6,
        out_specs=pl.BlockSpec(memory_space=pltpu.VMEM),
        scratch_shapes=[
            pltpu.VMEM((GROUP + 2 * SPAN, count), jnp.float32),
            pltpu.VMEM((POOL_B + 1, count, GROUP), jnp.bfloat16),
            pltpu.VMEM((POOL_A, GROUP, channels), jnp.bfloat16),
            pltpu.VMEM((count, channels), jnp.float32),
        ],
        cost_estimate=pl.CostEstimate(
            flops=20_000_000_000, bytes_accessed=4_000_000, transcendentals=1_600_000
        ),
        name="stem_stage",
    )(tokens, low, high, stem_weight, stem_bias, conv_gain)


def conv_kernel(count, ext_ref, weight_ref, bias_ref, coarse_ref):
    group = 4
    width = weight_ref.shape[-1]
    channels = ext_ref.shape[1]

    def block(m, carry):
        most, least = carry
        total = None
        for tap in range(KW):
            start = pl.multiple_of((m * group + tap) * count, count)
            part = jnp.dot(
                ext_ref[pl.ds(start, group * count), :],
                weight_ref[:, :, 0, tap].reshape(channels, width),
                preferred_element_type=jnp.float32,
            )
            total = part if total is None else total + part
        for index in range(group):
            piece = total[index * count : (index + 1) * count]
            most = jnp.maximum(most, piece)
            least = jnp.minimum(least, piece)
        return most, least

    big = jnp.full((count, width), jnp.finfo(jnp.float32).max, jnp.float32)
    most, least = lax.fori_loop(0, POOL_B // group, block, (-big, big))
    bias = bias_ref[...]
    coarse_ref[...] = jnp.maximum(jax.nn.gelu(most + bias), jax.nn.gelu(least + bias)).astype(
        jnp.bfloat16
    )


def conv_stage(ext, weight, conv_bias):
    count = ext.shape[0] // (POOL_B + 4)
    ways, row_parts, column_parts, taps, depth, columns = weight.shape
    width = 256
    steps = columns // width
    return pl.pallas_call(
        functools.partial(conv_kernel, count),
        grid=(column_parts, steps),
        out_shape=jax.ShapeDtypeStruct((count, column_parts * columns), jnp.bfloat16),
        in_specs=[
            pl.BlockSpec(ext.shape, lambda b, n: (0, 0), pipeline_mode=pl.Buffered(1)),
            pl.BlockSpec(
                (ways, row_parts, 1, taps, depth, width), lambda b, n: (0, 0, b, 0, 0, n)
            ),
            pl.BlockSpec((1, width), lambda b, n: (0, b * steps + n)),
        ],
        out_specs=pl.BlockSpec((count, width), lambda b, n: (0, b * steps + n)),
        cost_estimate=pl.CostEstimate(
            flops=24_000_000_000, bytes_accessed=16_000_000, transcendentals=400_000
        ),
        name="conv_stage",
    )(ext, weight, conv_bias[None])


MESH = pl.DeviceIdType.MESH


UNITS = 12
GROUPS = 3


def encoder_kernel(
    tok_ref,
    stem_weight_ref,
    stem_bias_ref,
    gain_ref,
    conv_bias_ref,
    attn_gain_ref,
    conv_ref,
    query_ref,
    keyw_ref,
    valuew_ref,
    outw_ref,
    out_ref,
    coarse_ref,
    key_ref,
    value_ref,
    text_ref,
    hot_ref,
    shifted_ref,
    rows_ref,
    turn_ref,
    ext_ref,
    low_ref,
    high_ref,
    conv_full,
    proj_full,
    outw_full,
    pair_send,
    pair_recv,
    halo_send,
    halo_recv,
    local_sem,
    recv_sem,
    partner_sem,
    x_sem,
    y_sem,
    partner_send,
    own_sem,
    relay_sem,
):
    wide = out_ref.shape[1]
    members = lax.axis_size("seq")
    me = lax.axis_index("dp")
    place = lax.axis_index("seq")
    chip = me // 2
    core = me % 2
    chips = lax.axis_size("dp") // 2
    partner = (chip * 2 + 1 - core, place)
    count = tok_ref.shape[0]
    depth, width = conv_full.shape[5:]
    unit_rows = proj_full.shape[1] // UNITS
    kinds = GROUPS + 2
    split = HEADS * HEAD_K
    middle = split + HEAD_K

    along_x = place + 1 - 2 * (place % 2)
    along_y = place + 2 - 4 * (place // 2)
    across = 3 - place
    mine = (place % 2 + place // 2) % 2
    theirs = 1 - mine
    x_target = (me, along_x)
    y_target = (me, along_y)

    sources = (1 + chip % 2, (chip + 2) % chips, 3 - 3 * (chip % 2))
    inner = (chip > 0) & (chip < chips - 1)
    relays = (3 * (chip - 1), None, chips - 1 - chip)

    first = (place, 4 + mine)
    x_out = ((0, place, None), (1, along_y, 1), (2, 4 + mine, 0))
    y_out = ((0, place, None), (1, along_x, 0), (2, 4 + mine, 1))
    x_in = ((0, along_x, None), (1, across, 1), (2, 4 + theirs, 0))
    y_in = ((0, along_y, None), (1, across, 0), (2, 4 + theirs, 1))

    def full_of(kind):
        return (*(conv_full.at[group] for group in range(GROUPS)), proj_full, outw_full)[kind]

    def part(kind, way, pair, half=None):
        full = full_of(kind).at[way]
        if kind < GROUPS:
            return full.at[pair] if half is None else full.at[pair, half]
        unit = 2 * pair + (half or 0)
        span = 2 if half is None else 1
        return full.at[pl.ds(pl.multiple_of(unit * unit_rows, unit_rows), span * unit_rows)]

    def remote(ref, send_sem, recv, target):
        return pltpu.make_async_remote_copy(ref, ref, send_sem, recv, target, MESH)

    def arrived(ref, recv):
        remote(ref, x_sem.at[0], recv, partner).wait_recv()

    def to_partner(kind, ref):
        remote(ref, partner_send.at[kind], partner_sem.at[kind], partner).start()

    def own(kind, i):
        ref = part(kind, me, first[i])
        recv = recv_sem.at[kind, chip, i]

        @pl.when(chip < chips - 1)
        def _():
            remote(ref, own_sem.at[kind, 0], recv, (me + 2, place)).start()

        @pl.when(chip > 0)
        def _():
            remote(ref, own_sem.at[kind, 1], recv, (me - 2, place)).start()

        @pl.when(jnp.logical_not(inner))
        def _():
            far = 2 * (chips - 1 - chip) + core
            remote(ref, own_sem.at[kind, 2], recv, (far, place)).start()

    def plane_send(kind, origin, k):
        way = 2 * origin + core
        for base, out, sem, target in ((2, x_out, x_sem, x_target), (5, y_out, y_sem, y_target)):
            k, pair, half = out[k]
            recv = recv_sem.at[kind, origin, base + k]
            remote(part(kind, way, pair, half), sem.at[kind], recv, target).start()

    def z_step(kind, i, j):
        origin = sources[j]
        ref = part(kind, 2 * origin + core, first[i])
        recv = recv_sem.at[kind, origin, i]
        arrived(ref, recv)
        if relays[j] is not None:

            @pl.when(inner)
            def _():
                remote(ref, relay_sem.at[kind, j // 2], recv, (2 * relays[j] + core, place)).start()

        plane_send(kind, origin, 2 * i)
        to_partner(kind, ref)

    def plane_step(kind, i, j):
        origin = sources[j]
        way = 2 * origin + core
        for ks in ((0,), (1, 2))[i : i + 1]:
            for k in ks:
                for base, into in ((2, x_in), (5, y_in)):
                    _, pair, half = into[k]
                    ref = part(kind, way, pair, half)
                    arrived(ref, recv_sem.at[kind, origin, base + k])
                    to_partner(kind, ref)
        if i == 0:
            plane_send(kind, origin, 1)

    stream = [(kind, i) for kind in range(kinds) for i in range(2)]
    events = []
    for turn in range(len(stream) + 1):
        for j in (0, 2, 1):
            at = turn - (j == 1)
            if 0 <= at < len(stream) and not (turn == len(stream) and j != 1):
                events.append((at, j))
    def event(n):
        if n < 100:
            at, j = events[n]
            z_step(*stream[at], j)
            if at == 1 and j == 0:
                own(*stream[2])
            if at > 0 and j == 2 and at + 2 < len(stream):
                own(*stream[at + 2])
        else:
            at, j = events[n - 100]
            plane_step(*stream[at], j)

    def run(*some):
        for n in some:
            event(n)

    def plane(*some):
        return [100 + n for n in some]

    def event_of(number, lists):
        for index, some in enumerate(lists):

            @pl.when(number == index)
            def _():
                run(*some)

    def local_copies(kind):
        if kind < GROUPS:
            for pair in range(UNITS // 2):
                for half in range(2):
                    rows = pl.ds(pair * depth, depth)
                    columns = pl.ds((2 * kind + half) * width, width)
                    yield conv_ref.at[:, rows, columns], part(kind, me, pair, half)
        elif kind == GROUPS:
            yield query_ref, proj_full.at[me, :, pl.ds(0, split)]
            yield keyw_ref, proj_full.at[me, :, pl.ds(split, HEAD_K)]
            yield valuew_ref, proj_full.at[me, :, pl.ds(middle, HEAD_V)]
        else:
            yield outw_ref, outw_full.at[me]

    def local_start(kind):
        for a, b in local_copies(kind):
            pltpu.make_async_copy(a, b, local_sem.at[kind]).start()

    def local_wait(kind):
        whole = full_of(kind).at[me]
        pltpu.make_async_copy(whole, whole, local_sem.at[kind]).wait()

    def own_partner(kind):
        to_partner(kind, full_of(kind).at[me])

    barrier = pltpu.get_barrier_semaphore()
    pl.semaphore_signal(barrier, inc=1, device_id=partner, device_id_type=MESH)
    for turn in (1, chips - 1):
        neighbour = (chip + turn) % chips * 2 + core
        pl.semaphore_signal(barrier, inc=1, device_id=(neighbour, place), device_id_type=MESH)
    for turn in range(1, members):
        pl.semaphore_signal(
            barrier, inc=1, device_id=(me, (place + turn) % members), device_id_type=MESH
        )
    local_start(0)
    local_wait(0)
    pl.semaphore_wait(barrier, members + 2)

    right = (place + 1) % members
    left = (place + members - 1) % members
    halo = [
        pltpu.make_async_remote_copy(
            tok_ref.at[count - 8 : count], low_ref, halo_send.at[0], halo_recv.at[0], (me, right), MESH
        ),
        pltpu.make_async_remote_copy(
            tok_ref.at[0:8], high_ref, halo_send.at[1], halo_recv.at[1], (me, left), MESH
        ),
    ]
    for copy in halo:
        copy.start()
    own(0, 0)
    stem_shift(stem_weight_ref, shifted_ref)
    own(0, 1)
    own_partner(0)
    for kind in range(1, kinds):
        local_start(kind)
    stem_inside(tok_ref, text_ref, hot_ref)

    half_dim = HEAD_K // 2
    lane = lax.broadcasted_iota(jnp.int32, (count, HEAD_K), 1)
    step = lane % half_dim
    freqs = jnp.exp(step.astype(jnp.float32) * (-math.log(10000.0) / half_dim))
    position = place * count + lax.broadcasted_iota(jnp.int32, (count, HEAD_K), 0)
    angles = position.astype(jnp.float32) * freqs
    turn_ref[0] = jnp.cos(angles)
    sine = jnp.sin(angles)
    turn_ref[1] = jnp.where(lane < half_dim, -sine, sine)

    def outside():
        for copy in halo:
            copy.wait()
        low = jnp.where(place > 0, low_ref[7:8], 0)
        high = jnp.where(place < members - 1, high_ref[0:1], 0)
        stem_outside(column_of(low, GROUP), column_of(high, GROUP), text_ref, hot_ref)

    def loaded():
        for kind in range(1, kinds):
            local_wait(kind)
        own_partner(1)

    def passed():
        for kind in range(2, kinds):
            own_partner(kind)

    early_events = [[n, *plane(*range(max(n - 2, 0), n - 1))] for n in range(7)]
    early_events += [[7, *plane(5), 8, *plane(6)], []]

    def stem_round(r, nothing):
        def block(step, nothing):
            j = (step + 1) % (POOL_B + 1)
            stem_block(j, stem_bias_ref, gain_ref, ext_ref, hot_ref, shifted_ref, rows_ref)
            return nothing

        lax.fori_loop(2 * r, 2 * r + 2 - r // 8, block, 0)
        pl.when(r == 1)(loaded)
        pl.when(r == 3)(outside)
        pl.when(r == 5)(passed)
        event_of(r, early_events)
        return nothing

    lax.fori_loop(0, POOL_B // 2 + 1, stem_round, 0)
    stem_edges(place, members - 1, ext_ref, rows_ref)

    group = 8
    channels = ext_ref.shape[1]
    big = jnp.full((count, width), jnp.finfo(jnp.float32).max, jnp.float32)

    def conv_panel(turn, half, after):
        weight_ref = conv_full.at[turn, :, :, half]

        def block(m, carry):
            most, least = carry
            weight = jnp.concatenate(
                [weight_ref[:, :, tap].reshape(channels, width) for tap in range(KW)], axis=0
            )
            rows = jnp.concatenate(
                [
                    ext_ref[pl.ds(pl.multiple_of((m * group + tap) * count, count), group * count), :]
                    for tap in range(KW)
                ],
                axis=1,
            )
            total = jnp.dot(rows, weight, preferred_element_type=jnp.float32)
            for index in range(group):
                piece = total[index * count : (index + 1) * count]
                most = jnp.maximum(most, piece)
                least = jnp.minimum(least, piece)
            after(m)
            return most, least

        most, least = lax.fori_loop(0, POOL_B // group, block, (-big, big))
        at = pl.multiple_of((2 * turn + half) * width, width)
        bias = conv_bias_ref[pl.ds(at, width)].reshape(1, width)
        coarse_ref[:, pl.ds(at, width)] = jnp.maximum(
            jax.nn.gelu(most + bias), jax.nn.gelu(least + bias)
        ).astype(jnp.bfloat16)

    late_events = [
        [10, 11, *plane(8)],
        [12, 13, *plane(9)],
        [14, *plane(10, 11)],
        [15, *plane(12)],
        [17, 18, *plane(14)],
        [19, *plane(15, 16)],
        [20, 21, *plane(17)],
        [22, *plane(18)],
        [24, *plane(20, 21)],
        [25, 26, *plane(22)],
        [27, *plane(23, 24)],
        [28, *plane(25)],
    ]
    between = [[9, *plane(7)], [16, *plane(13)], [23, *plane(19)]]

    def conv_turn(t, nothing):
        for turn in range(GROUPS):

            @pl.when(t == 2 * turn)
            def _():
                run(*between[turn])
                arrived(conv_full.at[turn, pl.ds(0, chips)], partner_sem.at[turn])

        conv_panel(t // 2, t % 2, lambda m: event_of(POOL_B // group * t + m, late_events))
        return nothing

    lax.fori_loop(0, 2 * GROUPS, conv_turn, 0)
    arrived(proj_full.at[pl.ds(0, chips)], partner_sem.at[GROUPS])

    def weight(begin, end):
        return proj_full[:, :, begin:end].reshape(wide, end - begin)

    def turned(head):
        return (head * turn_ref[0] + pltpu.roll(head, HEAD_K // 2, 1) * turn_ref[1]).astype(jnp.bfloat16)

    hidden = rms_scale(coarse_ref[...].astype(jnp.float32), attn_gain_ref[...].reshape(1, -1)).astype(
        jnp.bfloat16
    )
    key_ref[place] = turned(
        jnp.dot(hidden, weight(split, middle), preferred_element_type=jnp.float32)
    )
    value_ref[place] = jnp.dot(
        hidden, weight(middle, middle + HEAD_V), preferred_element_type=jnp.float32
    ).astype(jnp.bfloat16)
    pairs = []
    for turn in range(1, members):
        for index, ref in enumerate((key_ref, value_ref)):
            copy = pltpu.make_async_remote_copy(
                ref.at[place],
                ref.at[place],
                pair_send.at[index, turn],
                pair_recv.at[index, place],
                (me, (place + turn) % members),
                MESH,
            )
            copy.start()
            pairs.append(copy)
    query = jnp.dot(hidden, weight(0, split), preferred_element_type=jnp.float32)
    run(*plane(26), 29, *plane(27, 28))
    for turn in range(1, members):
        spot = (place + turn) % members
        for index, ref in enumerate((key_ref, value_ref)):
            arrived(ref.at[spot], pair_recv.at[index, spot])
    keys = key_ref[...].reshape(members * count, HEAD_K)
    values = value_ref[...].reshape(members * count, HEAD_V)
    mixes = []
    for head in range(HEADS):
        scores = lax.dot_general(
            turned(query[:, head * HEAD_K : (head + 1) * HEAD_K]),
            keys,
            (((1,), (1,)), ((), ())),
            preferred_element_type=jnp.float32,
        ) * HEAD_K ** (-0.5)
        raised = jnp.exp(scores - jnp.max(scores, axis=-1, keepdims=True))
        weights = (raised / jnp.sum(raised, axis=-1, keepdims=True)).astype(jnp.bfloat16)
        mixes.append(
            jnp.dot(weights, values, preferred_element_type=jnp.float32).astype(jnp.bfloat16)
        )
    run(*plane(29))
    arrived(outw_full.at[pl.ds(0, chips)], partner_sem.at[GROUPS + 1])
    total = coarse_ref[...].astype(jnp.float32)
    for head in range(HEADS):
        total = total + jnp.dot(mixes[head], outw_full[head], preferred_element_type=jnp.float32)
    out_ref[...] = total.astype(jnp.bfloat16)
    for copy in pairs:
        copy.wait_send()
    for kind in range(kinds):
        whole = full_of(kind).at[0]
        remote(whole, x_sem.at[kind], recv_sem.at[0, 0, 0], x_target).wait_send()
        remote(whole, y_sem.at[kind], recv_sem.at[0, 0, 0], y_target).wait_send()
        every = full_of(kind).at[pl.ds(0, chips)]
        remote(every, partner_send.at[kind], recv_sem.at[0, 0, 0], partner).wait_send()
        ref = full_of(kind).at[0, pl.ds(0, 2 if kind < GROUPS else 4 * unit_rows)]

        @pl.when(chip < chips - 1)
        def _():
            remote(ref, own_sem.at[kind, 0], recv_sem.at[0, 0, 0], partner).wait_send()

        @pl.when(chip > 0)
        def _():
            remote(ref, own_sem.at[kind, 1], recv_sem.at[0, 0, 0], partner).wait_send()

        @pl.when(jnp.logical_not(inner))
        def _():
            remote(ref, own_sem.at[kind, 2], recv_sem.at[0, 0, 0], partner).wait_send()

        @pl.when(inner)
        def _():
            for index in range(2):
                remote(ref, relay_sem.at[kind, index], recv_sem.at[0, 0, 0], partner).wait_send()


def fits(ways, members, conv_weight, w_query, w_out):
    taps, depth, columns = conv_weight.shape
    rows = w_out.shape[0]
    return (
        ways == 8
        and members == 4
        and columns == 2 * GROUPS * 256
        and depth == UNITS // 2 * 16
        and rows == HEAD_V
        and HEADS == ways
        and rows % (16 * UNITS) == 0
    )


def encoder_stage(
    tokens, stem_weight, vectors, conv_weight, w_query, w_key, w_value, w_out
):
    count = tokens.shape[0]
    channels = stem_weight.shape[1]
    taps, depth, columns = conv_weight.shape
    rows = w_out.shape[0]
    ways = lax.axis_size("dp")
    members = lax.axis_size("seq")
    chips = ways // 2
    vmem = pl.BlockSpec(memory_space=pltpu.VMEM)
    hbm = pl.BlockSpec(memory_space=pl.ANY)
    dma = pltpu.SemaphoreType.DMA
    kinds = GROUPS + 2
    return pl.pallas_call(
        encoder_kernel,
        out_shape=jax.ShapeDtypeStruct((count, columns), jnp.bfloat16),
        in_specs=[vmem] * 6 + [hbm] * 5,
        out_specs=vmem,
        scratch_shapes=[
            pltpu.VMEM((count, columns), jnp.bfloat16),
            pltpu.VMEM((members, count, HEAD_K), jnp.bfloat16),
            pltpu.VMEM((members, count, HEAD_V), jnp.bfloat16),
            pltpu.VMEM((GROUP + 2 * SPAN, count), jnp.float32),
            pltpu.VMEM((POOL_B + 1, count, GROUP), jnp.bfloat16),
            pltpu.VMEM((POOL_A, GROUP, channels), jnp.bfloat16),
            pltpu.VMEM((count, channels), jnp.float32),
            pltpu.VMEM((2, count, HEAD_K), jnp.float32),
            pltpu.VMEM(((POOL_B + 4) * count, channels), jnp.bfloat16),
            pltpu.VMEM((8, GROUP), jnp.int32),
            pltpu.VMEM((8, GROUP), jnp.int32),
            pltpu.VMEM(
                (GROUPS, ways, UNITS // 2, 2, taps, depth // 6, columns // (2 * GROUPS)), jnp.bfloat16
            ),
            pltpu.VMEM((ways, rows, HEADS * HEAD_K + HEAD_K + HEAD_V), jnp.bfloat16),
            pltpu.VMEM((ways, rows, columns), jnp.bfloat16),
            dma((2, members)),
            dma((2, members)),
            dma((2,)),
            dma((2,)),
            dma((kinds,)),
            dma((kinds, chips, 8)),
            dma((kinds,)),
            dma((kinds,)),
            dma((kinds,)),
            dma((kinds,)),
            dma((kinds, 3)),
            dma((kinds, 2)),
        ],
        compiler_params=pltpu.CompilerParams(
            collective_id=0, has_side_effects=True, vmem_limit_bytes=40 * 2**20
        ),
        name="encoder_stage",
    )(*(pltpu.with_memory_space_constraint(x, pltpu.HBM) for x in (tokens, stem_weight, *vectors, conv_weight, w_query, w_key, w_value, w_out)))


def gather_conv(conv_weight):
    taps, depth, columns = conv_weight.shape
    members = lax.axis_size("seq")
    place = lax.axis_index("seq")
    for row_parts in (2, 1, 3):
        column_parts = members // row_parts
        if members % row_parts or depth % (16 * row_parts) or columns % (256 * column_parts):
            continue
        depth_part = depth // row_parts
        column_part = columns // column_parts
        piece = lax.dynamic_slice(
            conv_weight,
            (0, place // column_parts * depth_part, place % column_parts * column_part),
            (taps, depth_part, column_part),
        )
        full = lax.all_gather(piece, ("dp", "seq"), axis=0, tiled=False)
        return full.reshape(-1, row_parts, column_parts, taps, depth_part, column_part)
    full = lax.all_gather(conv_weight, "dp", axis=0, tiled=False)
    return full[:, None, None]


def gather_rows(weight):
    members = lax.axis_size("seq")
    rows = weight.shape[0] // members
    piece = lax.dynamic_slice_in_dim(weight, lax.axis_index("seq") * rows, rows, axis=0)
    return lax.all_gather(piece, ("dp", "seq"), axis=0, tiled=True)


def body(
    tokens,
    stem_weight,
    stem_bias,
    conv_gain,
    conv_weight,
    conv_bias,
    attn_gain,
    w_query,
    w_key,
    w_value,
    w_out,
):
    seq_local = tokens.shape[1]
    rows_att = seq_local // GROUP
    tokens = tokens.reshape(rows_att, GROUP)
    size = lax.axis_size("seq")
    rows = w_out.shape[0]
    split = HEADS * HEAD_K
    if fits(lax.axis_size("dp"), size, conv_weight, w_query, w_out):
        return encoder_stage(
            tokens,
            stem_weight,
            [stem_bias, conv_gain, conv_bias, attn_gain],
            conv_weight,
            w_query,
            w_key,
            w_value,
            w_out,
        )[None]
    else:
        full_conv = gather_conv(conv_weight)
        projections = gather_rows(jnp.concatenate([w_query, w_key, w_value], axis=1))
        first_rows = projections[:, : split + HEAD_K]
        value_rows = projections[:, split + HEAD_K :]
        full_out = gather_rows(w_out)
        forward = [(i, i + 1) for i in range(size - 1)]
        backward = [(i + 1, i) for i in range(size - 1)]
        low = lax.ppermute(tokens[-1:], "seq", forward)
        high = lax.ppermute(tokens[:1], "seq", backward)
        ext = stem_stage(tokens, low, high, stem_weight, stem_bias, conv_gain)
        coarse = conv_stage(ext, full_conv, conv_bias)
    residual = coarse.astype(jnp.float32)
    hidden = rms_scale(residual, attn_gain).astype(jnp.bfloat16)
    projected = jnp.dot(hidden, first_rows, preferred_element_type=jnp.float32)
    query = projected[:, :split]
    keys = projected[:, split:]
    values = jnp.dot(hidden, value_rows, preferred_element_type=jnp.float32)
    half_dim = HEAD_K // 2
    freqs = 10000.0 ** (-jnp.arange(half_dim, dtype=jnp.float32) / half_dim)
    positions = lax.axis_index("seq") * rows_att + jnp.arange(rows_att, dtype=jnp.int32)
    angles = positions.astype(jnp.float32)[:, None] * freqs[None, :]
    query = rotate(query.reshape(rows_att, HEADS, HEAD_K), angles[:, None, :]).astype(jnp.bfloat16)
    keys = rotate(keys, angles).astype(jnp.bfloat16)
    pair = jnp.concatenate([keys, values.astype(jnp.bfloat16)], axis=1)
    pair = lax.all_gather(pair, "seq", axis=0, tiled=True)
    keys_all, values_all = pair[:, :HEAD_K], pair[:, HEAD_K:]
    scores = jnp.einsum(
        "rhd,kd->hrk", query, keys_all, preferred_element_type=jnp.float32
    ) * HEAD_K ** (-0.5)
    weights = jax.nn.softmax(scores, axis=-1).astype(jnp.bfloat16)
    mixed = jnp.einsum(
        "hrk,kd->rhd", weights, values_all, preferred_element_type=jnp.float32
    ).astype(jnp.bfloat16)
    mixed = mixed.reshape(rows_att, HEADS * HEAD_V)
    out = jnp.dot(mixed, full_out, preferred_element_type=jnp.float32)
    return (residual + out).astype(jnp.bfloat16)[None]


def solution(mesh):
    in_specs = (
        P("dp", "seq"),
        P(),
        P(),
        P(),
        P(None, "dp", None),
        P(),
        P(),
        P("dp", None),
        P("dp", None),
        P("dp", None),
        P("dp", None),
    )
    out_specs = P("dp", "seq", None)
    return jax.shard_map(body, mesh=mesh, in_specs=in_specs, out_specs=out_specs, check_vma=False)
```

```python
import functools
import math

import jax
import jax.numpy as jnp
from jax import lax
from jax.experimental import pallas as pl
from jax.experimental.pallas import tpu as pltpu
from jax.sharding import PartitionSpec as P

HEADS = 8
HEAD_K = 128
HEAD_V = 192
KW_STEM = 15
KW = 5
POOL_A = 8
POOL_B = 16
GROUP = POOL_A * POOL_B
SPAN = 24

epsilon = 1e-06


def rms_scale(values, gain):
    return values * lax.rsqrt(jnp.mean(values * values, axis=-1, keepdims=True) + epsilon) * gain


def rotate(values, angles):
    half_dim = values.shape[-1] // 2
    first = values[..., :half_dim]
    second = values[..., half_dim:]
    cosine = jnp.cos(angles)
    sine = jnp.sin(angles)
    return jnp.concatenate(
        [first * cosine - second * sine, second * cosine + first * sine], axis=-1
    )


def stem_kernel(
    tok_ref, low_ref, high_ref, weight_ref, bias_ref, gain_ref, ext_ref, text_ref, hot_ref, shifted_ref, rows_ref
):
    stem_compute(
        tok_ref,
        low_ref[...],
        high_ref[...],
        weight_ref,
        bias_ref,
        gain_ref,
        ext_ref,
        text_ref,
        hot_ref,
        shifted_ref,
        rows_ref,
    )


def stem_shift(weight_ref, shifted_ref):
    source = lax.broadcasted_iota(jnp.int32, (GROUP, weight_ref.shape[0]), 1)
    target = lax.broadcasted_iota(jnp.int32, (GROUP, weight_ref.shape[0]), 0)
    tap = source // 4
    base = source - 4 * tap
    for offset in range(POOL_A):
        pick = (target == base * SPAN + offset + tap + 1).astype(jnp.float32).astype(jnp.bfloat16)
        shifted_ref[offset] = jnp.dot(
            pick, weight_ref[...], preferred_element_type=jnp.float32
        ).astype(jnp.bfloat16)


def hot_of(span):
    planes = [(span == float(code)).astype(jnp.float32) for code in range(1, 5)]
    planes.append(jnp.zeros((GROUP - 4 * SPAN, span.shape[1]), jnp.float32))
    return jnp.concatenate(planes, axis=0).T.astype(jnp.bfloat16)


def stem_inside(tok_ref, text_ref, hot_ref):
    text_ref[SPAN : SPAN + GROUP, :] = tok_ref[...].astype(jnp.float32).T
    for j in range(1, POOL_B - 1):
        hot_ref[j] = hot_of(text_ref[8 * j + SPAN - 8 : 8 * j + 2 * SPAN - 8, :])


def stem_outside(low, high, text_ref, hot_ref):
    count = text_ref.shape[1]
    lane = lax.broadcasted_iota(jnp.int32, (SPAN, count), 1)
    before = low.astype(jnp.float32)
    after = high.astype(jnp.float32)
    text_ref[0:SPAN, :] = jnp.where(
        lane == 0, before[GROUP - SPAN :, :], pltpu.roll(text_ref[GROUP : GROUP + SPAN, :], 1, 1)
    )
    text_ref[SPAN + GROUP :, :] = jnp.where(
        lane == count - 1, after[:SPAN, :], pltpu.roll(text_ref[SPAN : 2 * SPAN, :], count - 1, 1)
    )
    for j in (0, POOL_B - 1):
        hot_ref[j] = hot_of(text_ref[8 * j + SPAN - 8 : 8 * j + 2 * SPAN - 8, :])
    edge = jnp.where(
        lane == 0,
        text_ref[0:SPAN, :],
        jnp.where(
            lane == 1,
            pltpu.roll(text_ref[8 : 8 + SPAN, :], 1, 1),
            jnp.where(
                lane == 2,
                pltpu.roll(text_ref[GROUP + SPAN - 8 : GROUP + 2 * SPAN - 8, :], 3, 1),
                pltpu.roll(text_ref[GROUP + SPAN : GROUP + 2 * SPAN, :], 4, 1),
            ),
        ),
    )
    hot_ref[POOL_B] = hot_of(edge)


def column_of(row, count):
    return jnp.broadcast_to(row.astype(jnp.float32), (8, count)).T[:, 0:1]


def stem_block(j, bias_ref, gain_ref, ext_ref, hot_ref, shifted_ref, rows_ref):
    count, channels = rows_ref.shape
    width = 256
    hot = hot_ref[j]
    for chunk in range(channels // width):
        columns = slice(chunk * width, (chunk + 1) * width)
        best = None
        for offset in range(POOL_A):
            stem = jnp.dot(hot, shifted_ref[offset, :, columns], preferred_element_type=jnp.float32)
            best = stem if best is None else jnp.maximum(best, stem)
        pooled = jax.nn.gelu(best + bias_ref[columns].reshape(1, width)).astype(jnp.bfloat16)
        rows_ref[:, columns] = pooled.astype(jnp.float32)
    pooled = rows_ref[...]
    start = pl.multiple_of((j + 2) * count, count)
    ext_ref[pl.ds(start, count), :] = rms_scale(pooled, gain_ref[...].reshape(1, channels)).astype(jnp.bfloat16)


def stem_edges(place, last_place, ext_ref, rows_ref):
    count, channels = rows_ref.shape
    edges = ext_ref[(POOL_B + 2) * count : (POOL_B + 3) * count, :].astype(jnp.float32)
    left_keep = (place > 0).astype(jnp.float32)
    right_keep = (place < last_place).astype(jnp.float32)
    spot = lax.broadcasted_iota(jnp.int32, (count, channels), 0)
    for index in range(2):
        inner = ext_ref[(POOL_B + index) * count : (POOL_B + index + 1) * count, :]
        moved = pltpu.roll(inner.astype(jnp.float32), 1, 0)
        ext_ref[index * count : (index + 1) * count, :] = jnp.where(
            spot == 0, edges[index : index + 1, :] * left_keep, moved
        ).astype(jnp.bfloat16)
        inner = ext_ref[(2 + index) * count : (3 + index) * count, :]
        moved = pltpu.roll(inner.astype(jnp.float32), count - 1, 0)
        at = POOL_B + 2 + index
        ext_ref[at * count : (at + 1) * count, :] = jnp.where(
            spot == count - 1, edges[2 + index : 3 + index, :] * right_keep, moved
        ).astype(jnp.bfloat16)


def stem_compute(
    tok_ref, low, high, weight_ref, bias_ref, gain_ref, ext_ref, text_ref, hot_ref, shifted_ref, rows_ref
):
    stem_shift(weight_ref, shifted_ref)
    stem_inside(tok_ref, text_ref, hot_ref)
    stem_outside(column_of(low, GROUP), column_of(high, GROUP), text_ref, hot_ref)

    def block(j, carry):
        stem_block(j, bias_ref, gain_ref, ext_ref, hot_ref, shifted_ref, rows_ref)
        return carry

    lax.fori_loop(0, POOL_B + 1, block, 0)
    stem_edges(lax.axis_index("seq"), lax.axis_size("seq") - 1, ext_ref, rows_ref)


def stem_stage(tokens, low, high, stem_weight, stem_bias, conv_gain):
    count = tokens.shape[0]
    channels = stem_weight.shape[1]
    return pl.pallas_call(
        stem_kernel,
        out_shape=jax.ShapeDtypeStruct(((POOL_B + 4) * count, channels), jnp.bfloat16),
        in_specs=[pl.BlockSpec(memory_space=pltpu.VMEM)] * 6,
        out_specs=pl.BlockSpec(memory_space=pltpu.VMEM),
        scratch_shapes=[
            pltpu.VMEM((GROUP + 2 * SPAN, count), jnp.float32),
            pltpu.VMEM((POOL_B + 1, count, GROUP), jnp.bfloat16),
            pltpu.VMEM((POOL_A, GROUP, channels), jnp.bfloat16),
            pltpu.VMEM((count, channels), jnp.float32),
        ],
        cost_estimate=pl.CostEstimate(
            flops=20_000_000_000, bytes_accessed=4_000_000, transcendentals=1_600_000
        ),
        name="stem_stage",
    )(tokens, low, high, stem_weight, stem_bias, conv_gain)


def conv_kernel(count, ext_ref, weight_ref, bias_ref, coarse_ref):
    group = 4
    width = weight_ref.shape[-1]
    channels = ext_ref.shape[1]

    def block(m, carry):
        most, least = carry
        total = None
        for tap in range(KW):
            start = pl.multiple_of((m * group + tap) * count, count)
            part = jnp.dot(
                ext_ref[pl.ds(start, group * count), :],
                weight_ref[:, :, 0, tap].reshape(channels, width),
                preferred_element_type=jnp.float32,
            )
            total = part if total is None else total + part
        for index in range(group):
            piece = total[index * count : (index + 1) * count]
            most = jnp.maximum(most, piece)
            least = jnp.minimum(least, piece)
        return most, least

    big = jnp.full((count, width), jnp.finfo(jnp.float32).max, jnp.float32)
    most, least = lax.fori_loop(0, POOL_B // group, block, (-big, big))
    bias = bias_ref[...]
    coarse_ref[...] = jnp.maximum(jax.nn.gelu(most + bias), jax.nn.gelu(least + bias)).astype(
        jnp.bfloat16
    )


def conv_stage(ext, weight, conv_bias):
    count = ext.shape[0] // (POOL_B + 4)
    ways, row_parts, column_parts, taps, depth, columns = weight.shape
    width = 256
    steps = columns // width
    return pl.pallas_call(
        functools.partial(conv_kernel, count),
        grid=(column_parts, steps),
        out_shape=jax.ShapeDtypeStruct((count, column_parts * columns), jnp.bfloat16),
        in_specs=[
            pl.BlockSpec(ext.shape, lambda b, n: (0, 0), pipeline_mode=pl.Buffered(1)),
            pl.BlockSpec(
                (ways, row_parts, 1, taps, depth, width), lambda b, n: (0, 0, b, 0, 0, n)
            ),
            pl.BlockSpec((1, width), lambda b, n: (0, b * steps + n)),
        ],
        out_specs=pl.BlockSpec((count, width), lambda b, n: (0, b * steps + n)),
        cost_estimate=pl.CostEstimate(
            flops=24_000_000_000, bytes_accessed=16_000_000, transcendentals=400_000
        ),
        name="conv_stage",
    )(ext, weight, conv_bias[None])


MESH = pl.DeviceIdType.MESH


UNITS = 12
GROUPS = 3


def encoder_kernel(
    tok_ref,
    stem_weight_ref,
    stem_bias_ref,
    gain_ref,
    conv_bias_ref,
    attn_gain_ref,
    conv_ref,
    query_ref,
    keyw_ref,
    valuew_ref,
    outw_ref,
    out_ref,
    coarse_ref,
    key_ref,
    value_ref,
    text_ref,
    hot_ref,
    shifted_ref,
    rows_ref,
    turn_ref,
    ext_ref,
    low_ref,
    high_ref,
    conv_full,
    proj_full,
    outw_full,
    pair_send,
    pair_recv,
    halo_send,
    halo_recv,
    local_sem,
    recv_sem,
    partner_sem,
    x_sem,
    y_sem,
    partner_send,
    own_sem,
    relay_sem,
):
    wide = out_ref.shape[1]
    members = lax.axis_size("seq")
    me = lax.axis_index("dp")
    place = lax.axis_index("seq")
    chip = me // 2
    core = me % 2
    chips = lax.axis_size("dp") // 2
    partner = (chip * 2 + 1 - core, place)
    count = tok_ref.shape[0]
    depth, width = conv_full.shape[5:]
    unit_rows = proj_full.shape[1] // UNITS
    kinds = GROUPS + 2
    split = HEADS * HEAD_K
    middle = split + HEAD_K

    along_x = place + 1 - 2 * (place % 2)
    along_y = place + 2 - 4 * (place // 2)
    across = 3 - place
    mine = (place % 2 + place // 2) % 2
    theirs = 1 - mine
    x_target = (me, along_x)
    y_target = (me, along_y)

    sources = (1 + chip % 2, (chip + 2) % chips, 3 - 3 * (chip % 2))
    inner = (chip > 0) & (chip < chips - 1)
    relays = (3 * (chip - 1), None, chips - 1 - chip)

    first = (place, 4 + mine)
    x_out = ((0, place, None), (1, along_y, 1), (2, 4 + mine, 0))
    y_out = ((0, place, None), (1, along_x, 0), (2, 4 + mine, 1))
    x_in = ((0, along_x, None), (1, across, 1), (2, 4 + theirs, 0))
    y_in = ((0, along_y, None), (1, across, 0), (2, 4 + theirs, 1))

    def full_of(kind):
        return (*(conv_full.at[group] for group in range(GROUPS)), proj_full, outw_full)[kind]

    def part(kind, way, pair, half=None):
        full = full_of(kind).at[way]
        if kind < GROUPS:
            return full.at[pair] if half is None else full.at[pair, half]
        unit = 2 * pair + (half or 0)
        span = 2 if half is None else 1
        return full.at[pl.ds(pl.multiple_of(unit * unit_rows, unit_rows), span * unit_rows)]

    def remote(ref, send_sem, recv, target):
        return pltpu.make_async_remote_copy(ref, ref, send_sem, recv, target, MESH)

    def arrived(ref, recv):
        remote(ref, x_sem.at[0], recv, partner).wait_recv()

    def to_partner(kind, ref):
        remote(ref, partner_send.at[kind], partner_sem.at[kind], partner).start()

    def own(kind, i):
        ref = part(kind, me, first[i])
        recv = recv_sem.at[kind, chip, i]

        @pl.when(chip < chips - 1)
        def _():
            remote(ref, own_sem.at[kind, 0], recv, (me + 2, place)).start()

        @pl.when(chip > 0)
        def _():
            remote(ref, own_sem.at[kind, 1], recv, (me - 2, place)).start()

        @pl.when(jnp.logical_not(inner))
        def _():
            far = 2 * (chips - 1 - chip) + core
            remote(ref, own_sem.at[kind, 2], recv, (far, place)).start()

    def plane_send(kind, origin, k):
        way = 2 * origin + core
        for base, out, sem, target in ((2, x_out, x_sem, x_target), (5, y_out, y_sem, y_target)):
            k, pair, half = out[k]
            recv = recv_sem.at[kind, origin, base + k]
            remote(part(kind, way, pair, half), sem.at[kind], recv, target).start()

    def z_step(kind, i, j):
        origin = sources[j]
        ref = part(kind, 2 * origin + core, first[i])
        recv = recv_sem.at[kind, origin, i]
        arrived(ref, recv)
        if relays[j] is not None:

            @pl.when(inner)
            def _():
                remote(ref, relay_sem.at[kind, j // 2], recv, (2 * relays[j] + core, place)).start()

        plane_send(kind, origin, 2 * i)
        to_partner(kind, ref)

    def plane_step(kind, i, j):
        origin = sources[j]
        way = 2 * origin + core
        for ks in ((0,), (1, 2))[i : i + 1]:
            for k in ks:
                for base, into in ((2, x_in), (5, y_in)):
                    _, pair, half = into[k]
                    ref = part(kind, way, pair, half)
                    arrived(ref, recv_sem.at[kind, origin, base + k])
                    to_partner(kind, ref)
        if i == 0:
            plane_send(kind, origin, 1)

    stream = [(kind, i) for kind in range(kinds) for i in range(2)]
    events = []
    for turn in range(len(stream) + 1):
        for j in (0, 2, 1):
            at = turn - (j == 1)
            if 0 <= at < len(stream) and not (turn == len(stream) and j != 1):
                events.append((at, j))
    def event(n):
        if n < 100:
            at, j = events[n]
            z_step(*stream[at], j)
            if at == 1 and j == 0:
                own(*stream[2])
            if at > 0 and j == 2 and at + 2 < len(stream):
                own(*stream[at + 2])
        else:
            at, j = events[n - 100]
            plane_step(*stream[at], j)

    def run(*some):
        for n in some:
            event(n)

    def plane(*some):
        return [100 + n for n in some]

    def event_of(number, lists):
        for index, some in enumerate(lists):

            @pl.when(number == index)
            def _():
                run(*some)

    def local_copies(kind):
        if kind < GROUPS:
            for pair in range(UNITS // 2):
                for half in range(2):
                    rows = pl.ds(pair * depth, depth)
                    columns = pl.ds((2 * kind + half) * width, width)
                    yield conv_ref.at[:, rows, columns], part(kind, me, pair, half)
        elif kind == GROUPS:
            yield query_ref, proj_full.at[me, :, pl.ds(0, split)]
            yield keyw_ref, proj_full.at[me, :, pl.ds(split, HEAD_K)]
            yield valuew_ref, proj_full.at[me, :, pl.ds(middle, HEAD_V)]
        else:
            yield outw_ref, outw_full.at[me]

    def local_start(kind):
        for a, b in local_copies(kind):
            pltpu.make_async_copy(a, b, local_sem.at[kind]).start()

    def local_wait(kind):
        whole = full_of(kind).at[me]
        pltpu.make_async_copy(whole, whole, local_sem.at[kind]).wait()

    def own_partner(kind):
        to_partner(kind, full_of(kind).at[me])

    barrier = pltpu.get_barrier_semaphore()
    pl.semaphore_signal(barrier, inc=1, device_id=partner, device_id_type=MESH)
    for turn in (1, chips - 1):
        neighbour = (chip + turn) % chips * 2 + core
        pl.semaphore_signal(barrier, inc=1, device_id=(neighbour, place), device_id_type=MESH)
    for turn in range(1, members):
        pl.semaphore_signal(
            barrier, inc=1, device_id=(me, (place + turn) % members), device_id_type=MESH
        )
    local_start(0)
    local_wait(0)
    pl.semaphore_wait(barrier, members + 2)

    right = (place + 1) % members
    left = (place + members - 1) % members
    halo = [
        pltpu.make_async_remote_copy(
            tok_ref.at[count - 8 : count], low_ref, halo_send.at[0], halo_recv.at[0], (me, right), MESH
        ),
        pltpu.make_async_remote_copy(
            tok_ref.at[0:8], high_ref, halo_send.at[1], halo_recv.at[1], (me, left), MESH
        ),
    ]
    for copy in halo:
        copy.start()
    own(0, 0)
    stem_shift(stem_weight_ref, shifted_ref)
    own(0, 1)
    own_partner(0)
    for kind in range(1, kinds):
        local_start(kind)
    stem_inside(tok_ref, text_ref, hot_ref)

    half_dim = HEAD_K // 2
    lane = lax.broadcasted_iota(jnp.int32, (count, HEAD_K), 1)
    step = lane % half_dim
    freqs = jnp.exp(step.astype(jnp.float32) * (-math.log(10000.0) / half_dim))
    position = place * count + lax.broadcasted_iota(jnp.int32, (count, HEAD_K), 0)
    angles = position.astype(jnp.float32) * freqs
    turn_ref[0] = jnp.cos(angles)
    sine = jnp.sin(angles)
    turn_ref[1] = jnp.where(lane < half_dim, -sine, sine)

    def outside():
        for copy in halo:
            copy.wait()
        low = jnp.where(place > 0, low_ref[7:8], 0)
        high = jnp.where(place < members - 1, high_ref[0:1], 0)
        stem_outside(column_of(low, GROUP), column_of(high, GROUP), text_ref, hot_ref)

    def loaded():
        for kind in range(1, kinds):
            local_wait(kind)
        own_partner(1)

    def passed():
        for kind in range(2, kinds):
            own_partner(kind)

    inner_events = [[n, *plane(*range(max(n - 2, 0), n - 1))] for n in range(7)]
    inner_events += [[7, *plane(5), 8, *plane(6)], []]
    outer_events = inner_events[:5] + [[7, *plane(3)], [*plane(4)], [5, *plane(7), 6], [8, *plane(5)]]

    def stem_round(r, nothing):
        def block(step, nothing):
            j = (step + 1) % (POOL_B + 1)
            stem_block(j, stem_bias_ref, gain_ref, ext_ref, hot_ref, shifted_ref, rows_ref)
            return nothing

        lax.fori_loop(2 * r, 2 * r + 2 - r // 8, block, 0)
        pl.when(r == 1)(loaded)
        pl.when(r == 3)(outside)
        pl.when(r == 5)(passed)

        @pl.when(inner)
        def _():
            event_of(r, inner_events)

        @pl.when(jnp.logical_not(inner))
        def _():
            event_of(r, outer_events)

        return nothing

    lax.fori_loop(0, POOL_B // 2 + 1, stem_round, 0)
    stem_edges(place, members - 1, ext_ref, rows_ref)

    group = 8
    channels = ext_ref.shape[1]
    big = jnp.full((count, width), jnp.finfo(jnp.float32).max, jnp.float32)

    def conv_panel(turn, half, after):
        weight_ref = conv_full.at[turn, :, :, half]

        def block(m, carry):
            most, least = carry
            weight = jnp.concatenate(
                [weight_ref[:, :, tap].reshape(channels, width) for tap in range(KW)], axis=0
            )
            rows = jnp.concatenate(
                [
                    ext_ref[pl.ds(pl.multiple_of((m * group + tap) * count, count), group * count), :]
                    for tap in range(KW)
                ],
                axis=1,
            )
            total = jnp.dot(rows, weight, preferred_element_type=jnp.float32)
            for index in range(group):
                piece = total[index * count : (index + 1) * count]
                most = jnp.maximum(most, piece)
                least = jnp.minimum(least, piece)
            after(m)
            return most, least

        most, least = lax.fori_loop(0, POOL_B // group, block, (-big, big))
        at = pl.multiple_of((2 * turn + half) * width, width)
        bias = conv_bias_ref[pl.ds(at, width)].reshape(1, width)
        coarse_ref[:, pl.ds(at, width)] = jnp.maximum(
            jax.nn.gelu(most + bias), jax.nn.gelu(least + bias)
        ).astype(jnp.bfloat16)

    late_events = [
        [10, 11, *plane(8)],
        [12, 13, *plane(9)],
        [14, *plane(10, 11)],
        [15, *plane(12)],
        [17, 18, *plane(14)],
        [19, *plane(15, 16)],
        [20, 21, *plane(17)],
        [22, *plane(18)],
        [24, *plane(20, 21)],
        [25, 26, *plane(22)],
        [27, *plane(23, 24)],
        [28, *plane(25)],
    ]
    between = [[9], [16, *plane(13)], [23, *plane(19)]]
    pl.when(inner)(lambda: run(*plane(7)))
    pl.when(jnp.logical_not(inner))(lambda: run(*plane(6)))

    def conv_turn(t, nothing):
        for turn in range(GROUPS):

            @pl.when(t == 2 * turn)
            def _():
                run(*between[turn])
                arrived(conv_full.at[turn, pl.ds(0, chips)], partner_sem.at[turn])

        conv_panel(t // 2, t % 2, lambda m: event_of(POOL_B // group * t + m, late_events))
        return nothing

    lax.fori_loop(0, 2 * GROUPS, conv_turn, 0)
    arrived(proj_full.at[pl.ds(0, chips)], partner_sem.at[GROUPS])

    def weight(begin, end):
        return proj_full[:, :, begin:end].reshape(wide, end - begin)

    def turned(head):
        return (head * turn_ref[0] + pltpu.roll(head, HEAD_K // 2, 1) * turn_ref[1]).astype(jnp.bfloat16)

    hidden = rms_scale(coarse_ref[...].astype(jnp.float32), attn_gain_ref[...].reshape(1, -1)).astype(
        jnp.bfloat16
    )
    key_ref[place] = turned(
        jnp.dot(hidden, weight(split, middle), preferred_element_type=jnp.float32)
    )
    value_ref[place] = jnp.dot(
        hidden, weight(middle, middle + HEAD_V), preferred_element_type=jnp.float32
    ).astype(jnp.bfloat16)
    pairs = []
    for turn in range(1, members):
        for index, ref in enumerate((key_ref, value_ref)):
            copy = pltpu.make_async_remote_copy(
                ref.at[place],
                ref.at[place],
                pair_send.at[index, turn],
                pair_recv.at[index, place],
                (me, (place + turn) % members),
                MESH,
            )
            copy.start()
            pairs.append(copy)
    query = jnp.dot(hidden, weight(0, split), preferred_element_type=jnp.float32)
    run(*plane(26), 29, *plane(27, 28))
    for turn in range(1, members):
        spot = (place + turn) % members
        for index, ref in enumerate((key_ref, value_ref)):
            arrived(ref.at[spot], pair_recv.at[index, spot])
    keys = key_ref[...].reshape(members * count, HEAD_K)
    values = value_ref[...].reshape(members * count, HEAD_V)
    mixes = []
    for head in range(HEADS):
        scores = lax.dot_general(
            turned(query[:, head * HEAD_K : (head + 1) * HEAD_K]),
            keys,
            (((1,), (1,)), ((), ())),
            preferred_element_type=jnp.float32,
        ) * HEAD_K ** (-0.5)
        raised = jnp.exp(scores - jnp.max(scores, axis=-1, keepdims=True))
        weights = (raised / jnp.sum(raised, axis=-1, keepdims=True)).astype(jnp.bfloat16)
        mixes.append(
            jnp.dot(weights, values, preferred_element_type=jnp.float32).astype(jnp.bfloat16)
        )
    run(*plane(29))
    arrived(outw_full.at[pl.ds(0, chips)], partner_sem.at[GROUPS + 1])
    total = coarse_ref[...].astype(jnp.float32)
    for head in range(HEADS):
        total = total + jnp.dot(mixes[head], outw_full[head], preferred_element_type=jnp.float32)
    out_ref[...] = total.astype(jnp.bfloat16)
    for copy in pairs:
        copy.wait_send()
    for kind in range(kinds):
        whole = full_of(kind).at[0]
        remote(whole, x_sem.at[kind], recv_sem.at[0, 0, 0], x_target).wait_send()
        remote(whole, y_sem.at[kind], recv_sem.at[0, 0, 0], y_target).wait_send()
        every = full_of(kind).at[pl.ds(0, chips)]
        remote(every, partner_send.at[kind], recv_sem.at[0, 0, 0], partner).wait_send()
        ref = full_of(kind).at[0, pl.ds(0, 2 if kind < GROUPS else 4 * unit_rows)]

        @pl.when(chip < chips - 1)
        def _():
            remote(ref, own_sem.at[kind, 0], recv_sem.at[0, 0, 0], partner).wait_send()

        @pl.when(chip > 0)
        def _():
            remote(ref, own_sem.at[kind, 1], recv_sem.at[0, 0, 0], partner).wait_send()

        @pl.when(jnp.logical_not(inner))
        def _():
            remote(ref, own_sem.at[kind, 2], recv_sem.at[0, 0, 0], partner).wait_send()

        @pl.when(inner)
        def _():
            for index in range(2):
                remote(ref, relay_sem.at[kind, index], recv_sem.at[0, 0, 0], partner).wait_send()


def fits(ways, members, conv_weight, w_query, w_out):
    taps, depth, columns = conv_weight.shape
    rows = w_out.shape[0]
    return (
        ways == 8
        and members == 4
        and columns == 2 * GROUPS * 256
        and depth == UNITS // 2 * 16
        and rows == HEAD_V
        and HEADS == ways
        and rows % (16 * UNITS) == 0
    )


def encoder_stage(
    tokens, stem_weight, vectors, conv_weight, w_query, w_key, w_value, w_out
):
    count = tokens.shape[0]
    channels = stem_weight.shape[1]
    taps, depth, columns = conv_weight.shape
    rows = w_out.shape[0]
    ways = lax.axis_size("dp")
    members = lax.axis_size("seq")
    chips = ways // 2
    vmem = pl.BlockSpec(memory_space=pltpu.VMEM)
    hbm = pl.BlockSpec(memory_space=pl.ANY)
    dma = pltpu.SemaphoreType.DMA
    kinds = GROUPS + 2
    return pl.pallas_call(
        encoder_kernel,
        out_shape=jax.ShapeDtypeStruct((count, columns), jnp.bfloat16),
        in_specs=[vmem] * 6 + [hbm] * 5,
        out_specs=vmem,
        scratch_shapes=[
            pltpu.VMEM((count, columns), jnp.bfloat16),
            pltpu.VMEM((members, count, HEAD_K), jnp.bfloat16),
            pltpu.VMEM((members, count, HEAD_V), jnp.bfloat16),
            pltpu.VMEM((GROUP + 2 * SPAN, count), jnp.float32),
            pltpu.VMEM((POOL_B + 1, count, GROUP), jnp.bfloat16),
            pltpu.VMEM((POOL_A, GROUP, channels), jnp.bfloat16),
            pltpu.VMEM((count, channels), jnp.float32),
            pltpu.VMEM((2, count, HEAD_K), jnp.float32),
            pltpu.VMEM(((POOL_B + 4) * count, channels), jnp.bfloat16),
            pltpu.VMEM((8, GROUP), jnp.int32),
            pltpu.VMEM((8, GROUP), jnp.int32),
            pltpu.VMEM(
                (GROUPS, ways, UNITS // 2, 2, taps, depth // 6, columns // (2 * GROUPS)), jnp.bfloat16
            ),
            pltpu.VMEM((ways, rows, HEADS * HEAD_K + HEAD_K + HEAD_V), jnp.bfloat16),
            pltpu.VMEM((ways, rows, columns), jnp.bfloat16),
            dma((2, members)),
            dma((2, members)),
            dma((2,)),
            dma((2,)),
            dma((kinds,)),
            dma((kinds, chips, 8)),
            dma((kinds,)),
            dma((kinds,)),
            dma((kinds,)),
            dma((kinds,)),
            dma((kinds, 3)),
            dma((kinds, 2)),
        ],
        compiler_params=pltpu.CompilerParams(
            collective_id=0, has_side_effects=True, vmem_limit_bytes=40 * 2**20
        ),
        name="encoder_stage",
    )(*(pltpu.with_memory_space_constraint(x, pltpu.HBM) for x in (tokens, stem_weight, *vectors, conv_weight, w_query, w_key, w_value, w_out)))


def gather_conv(conv_weight):
    taps, depth, columns = conv_weight.shape
    members = lax.axis_size("seq")
    place = lax.axis_index("seq")
    for row_parts in (2, 1, 3):
        column_parts = members // row_parts
        if members % row_parts or depth % (16 * row_parts) or columns % (256 * column_parts):
            continue
        depth_part = depth // row_parts
        column_part = columns // column_parts
        piece = lax.dynamic_slice(
            conv_weight,
            (0, place // column_parts * depth_part, place % column_parts * column_part),
            (taps, depth_part, column_part),
        )
        full = lax.all_gather(piece, ("dp", "seq"), axis=0, tiled=False)
        return full.reshape(-1, row_parts, column_parts, taps, depth_part, column_part)
    full = lax.all_gather(conv_weight, "dp", axis=0, tiled=False)
    return full[:, None, None]


def gather_rows(weight):
    members = lax.axis_size("seq")
    rows = weight.shape[0] // members
    piece = lax.dynamic_slice_in_dim(weight, lax.axis_index("seq") * rows, rows, axis=0)
    return lax.all_gather(piece, ("dp", "seq"), axis=0, tiled=True)


def body(
    tokens,
    stem_weight,
    stem_bias,
    conv_gain,
    conv_weight,
    conv_bias,
    attn_gain,
    w_query,
    w_key,
    w_value,
    w_out,
):
    seq_local = tokens.shape[1]
    rows_att = seq_local // GROUP
    tokens = tokens.reshape(rows_att, GROUP)
    size = lax.axis_size("seq")
    rows = w_out.shape[0]
    split = HEADS * HEAD_K
    if fits(lax.axis_size("dp"), size, conv_weight, w_query, w_out):
        return encoder_stage(
            tokens,
            stem_weight,
            [stem_bias, conv_gain, conv_bias, attn_gain],
            conv_weight,
            w_query,
            w_key,
            w_value,
            w_out,
        )[None]
    else:
        full_conv = gather_conv(conv_weight)
        projections = gather_rows(jnp.concatenate([w_query, w_key, w_value], axis=1))
        first_rows = projections[:, : split + HEAD_K]
        value_rows = projections[:, split + HEAD_K :]
        full_out = gather_rows(w_out)
        forward = [(i, i + 1) for i in range(size - 1)]
        backward = [(i + 1, i) for i in range(size - 1)]
        low = lax.ppermute(tokens[-1:], "seq", forward)
        high = lax.ppermute(tokens[:1], "seq", backward)
        ext = stem_stage(tokens, low, high, stem_weight, stem_bias, conv_gain)
        coarse = conv_stage(ext, full_conv, conv_bias)
    residual = coarse.astype(jnp.float32)
    hidden = rms_scale(residual, attn_gain).astype(jnp.bfloat16)
    projected = jnp.dot(hidden, first_rows, preferred_element_type=jnp.float32)
    query = projected[:, :split]
    keys = projected[:, split:]
    values = jnp.dot(hidden, value_rows, preferred_element_type=jnp.float32)
    half_dim = HEAD_K // 2
    freqs = 10000.0 ** (-jnp.arange(half_dim, dtype=jnp.float32) / half_dim)
    positions = lax.axis_index("seq") * rows_att + jnp.arange(rows_att, dtype=jnp.int32)
    angles = positions.astype(jnp.float32)[:, None] * freqs[None, :]
    query = rotate(query.reshape(rows_att, HEADS, HEAD_K), angles[:, None, :]).astype(jnp.bfloat16)
    keys = rotate(keys, angles).astype(jnp.bfloat16)
    pair = jnp.concatenate([keys, values.astype(jnp.bfloat16)], axis=1)
    pair = lax.all_gather(pair, "seq", axis=0, tiled=True)
    keys_all, values_all = pair[:, :HEAD_K], pair[:, HEAD_K:]
    scores = jnp.einsum(
        "rhd,kd->hrk", query, keys_all, preferred_element_type=jnp.float32
    ) * HEAD_K ** (-0.5)
    weights = jax.nn.softmax(scores, axis=-1).astype(jnp.bfloat16)
    mixed = jnp.einsum(
        "hrk,kd->rhd", weights, values_all, preferred_element_type=jnp.float32
    ).astype(jnp.bfloat16)
    mixed = mixed.reshape(rows_att, HEADS * HEAD_V)
    out = jnp.dot(mixed, full_out, preferred_element_type=jnp.float32)
    return (residual + out).astype(jnp.bfloat16)[None]


def solution(mesh):
    in_specs = (
        P("dp", "seq"),
        P(),
        P(),
        P(),
        P(None, "dp", None),
        P(),
        P(),
        P("dp", None),
        P("dp", None),
        P("dp", None),
        P("dp", None),
    )
    out_specs = P("dp", "seq", None)
    return jax.shard_map(body, mesh=mesh, in_specs=in_specs, out_specs=out_specs, check_vma=False)
```

```python
import functools
import math

import jax
import jax.numpy as jnp
from jax import lax
from jax.experimental import pallas as pl
from jax.experimental.pallas import tpu as pltpu
from jax.sharding import PartitionSpec as P

HEADS = 8
HEAD_K = 128
HEAD_V = 192
KW_STEM = 15
KW = 5
POOL_A = 8
POOL_B = 16
GROUP = POOL_A * POOL_B
SPAN = 24

epsilon = 1e-06


def rms_scale(values, gain):
    return values * lax.rsqrt(jnp.mean(values * values, axis=-1, keepdims=True) + epsilon) * gain


def rotate(values, angles):
    half_dim = values.shape[-1] // 2
    first = values[..., :half_dim]
    second = values[..., half_dim:]
    cosine = jnp.cos(angles)
    sine = jnp.sin(angles)
    return jnp.concatenate(
        [first * cosine - second * sine, second * cosine + first * sine], axis=-1
    )


def stem_kernel(
    tok_ref, low_ref, high_ref, weight_ref, bias_ref, gain_ref, ext_ref, text_ref, hot_ref, shifted_ref, rows_ref
):
    stem_compute(
        tok_ref,
        low_ref[...],
        high_ref[...],
        weight_ref,
        bias_ref,
        gain_ref,
        ext_ref,
        text_ref,
        hot_ref,
        shifted_ref,
        rows_ref,
    )


def stem_shift(weight_ref, shifted_ref):
    source = lax.broadcasted_iota(jnp.int32, (GROUP, weight_ref.shape[0]), 1)
    target = lax.broadcasted_iota(jnp.int32, (GROUP, weight_ref.shape[0]), 0)
    tap = source // 4
    base = source - 4 * tap
    for offset in range(POOL_A):
        pick = (target == base * SPAN + offset + tap + 1).astype(jnp.float32).astype(jnp.bfloat16)
        shifted_ref[offset] = jnp.dot(
            pick, weight_ref[...], preferred_element_type=jnp.float32
        ).astype(jnp.bfloat16)


def hot_of(span):
    planes = [(span == float(code)).astype(jnp.float32) for code in range(1, 5)]
    planes.append(jnp.zeros((GROUP - 4 * SPAN, span.shape[1]), jnp.float32))
    return jnp.concatenate(planes, axis=0).T.astype(jnp.bfloat16)


def stem_inside(tok_ref, text_ref, hot_ref):
    text_ref[SPAN : SPAN + GROUP, :] = tok_ref[...].astype(jnp.float32).T
    for j in range(1, POOL_B - 1):
        hot_ref[j] = hot_of(text_ref[8 * j + SPAN - 8 : 8 * j + 2 * SPAN - 8, :])


def stem_outside(low, high, text_ref, hot_ref):
    count = text_ref.shape[1]
    lane = lax.broadcasted_iota(jnp.int32, (SPAN, count), 1)
    before = low.astype(jnp.float32)
    after = high.astype(jnp.float32)
    text_ref[0:SPAN, :] = jnp.where(
        lane == 0, before[GROUP - SPAN :, :], pltpu.roll(text_ref[GROUP : GROUP + SPAN, :], 1, 1)
    )
    text_ref[SPAN + GROUP :, :] = jnp.where(
        lane == count - 1, after[:SPAN, :], pltpu.roll(text_ref[SPAN : 2 * SPAN, :], count - 1, 1)
    )
    for j in (0, POOL_B - 1):
        hot_ref[j] = hot_of(text_ref[8 * j + SPAN - 8 : 8 * j + 2 * SPAN - 8, :])
    edge = jnp.where(
        lane == 0,
        text_ref[0:SPAN, :],
        jnp.where(
            lane == 1,
            pltpu.roll(text_ref[8 : 8 + SPAN, :], 1, 1),
            jnp.where(
                lane == 2,
                pltpu.roll(text_ref[GROUP + SPAN - 8 : GROUP + 2 * SPAN - 8, :], 3, 1),
                pltpu.roll(text_ref[GROUP + SPAN : GROUP + 2 * SPAN, :], 4, 1),
            ),
        ),
    )
    hot_ref[POOL_B] = hot_of(edge)


def column_of(row, count):
    return jnp.broadcast_to(row.astype(jnp.float32), (8, count)).T[:, 0:1]


def stem_block(j, bias_ref, gain_ref, ext_ref, hot_ref, shifted_ref, rows_ref):
    count, channels = rows_ref.shape
    width = 256
    hot = hot_ref[j]
    for chunk in range(channels // width):
        columns = slice(chunk * width, (chunk + 1) * width)
        best = None
        for offset in range(POOL_A):
            stem = jnp.dot(hot, shifted_ref[offset, :, columns], preferred_element_type=jnp.float32)
            best = stem if best is None else jnp.maximum(best, stem)
        pooled = jax.nn.gelu(best + bias_ref[columns].reshape(1, width)).astype(jnp.bfloat16)
        rows_ref[:, columns] = pooled.astype(jnp.float32)
    pooled = rows_ref[...]
    start = pl.multiple_of((j + 2) * count, count)
    ext_ref[pl.ds(start, count), :] = rms_scale(pooled, gain_ref[...].reshape(1, channels)).astype(jnp.bfloat16)


def stem_edges(place, last_place, ext_ref, rows_ref):
    count, channels = rows_ref.shape
    edges = ext_ref[(POOL_B + 2) * count : (POOL_B + 3) * count, :].astype(jnp.float32)
    left_keep = (place > 0).astype(jnp.float32)
    right_keep = (place < last_place).astype(jnp.float32)
    spot = lax.broadcasted_iota(jnp.int32, (count, channels), 0)
    for index in range(2):
        inner = ext_ref[(POOL_B + index) * count : (POOL_B + index + 1) * count, :]
        moved = pltpu.roll(inner.astype(jnp.float32), 1, 0)
        ext_ref[index * count : (index + 1) * count, :] = jnp.where(
            spot == 0, edges[index : index + 1, :] * left_keep, moved
        ).astype(jnp.bfloat16)
        inner = ext_ref[(2 + index) * count : (3 + index) * count, :]
        moved = pltpu.roll(inner.astype(jnp.float32), count - 1, 0)
        at = POOL_B + 2 + index
        ext_ref[at * count : (at + 1) * count, :] = jnp.where(
            spot == count - 1, edges[2 + index : 3 + index, :] * right_keep, moved
        ).astype(jnp.bfloat16)


def stem_compute(
    tok_ref, low, high, weight_ref, bias_ref, gain_ref, ext_ref, text_ref, hot_ref, shifted_ref, rows_ref
):
    stem_shift(weight_ref, shifted_ref)
    stem_inside(tok_ref, text_ref, hot_ref)
    stem_outside(column_of(low, GROUP), column_of(high, GROUP), text_ref, hot_ref)

    def block(j, carry):
        stem_block(j, bias_ref, gain_ref, ext_ref, hot_ref, shifted_ref, rows_ref)
        return carry

    lax.fori_loop(0, POOL_B + 1, block, 0)
    stem_edges(lax.axis_index("seq"), lax.axis_size("seq") - 1, ext_ref, rows_ref)


def stem_stage(tokens, low, high, stem_weight, stem_bias, conv_gain):
    count = tokens.shape[0]
    channels = stem_weight.shape[1]
    return pl.pallas_call(
        stem_kernel,
        out_shape=jax.ShapeDtypeStruct(((POOL_B + 4) * count, channels), jnp.bfloat16),
        in_specs=[pl.BlockSpec(memory_space=pltpu.VMEM)] * 6,
        out_specs=pl.BlockSpec(memory_space=pltpu.VMEM),
        scratch_shapes=[
            pltpu.VMEM((GROUP + 2 * SPAN, count), jnp.float32),
            pltpu.VMEM((POOL_B + 1, count, GROUP), jnp.bfloat16),
            pltpu.VMEM((POOL_A, GROUP, channels), jnp.bfloat16),
            pltpu.VMEM((count, channels), jnp.float32),
        ],
        cost_estimate=pl.CostEstimate(
            flops=20_000_000_000, bytes_accessed=4_000_000, transcendentals=1_600_000
        ),
        name="stem_stage",
    )(tokens, low, high, stem_weight, stem_bias, conv_gain)


def conv_kernel(count, ext_ref, weight_ref, bias_ref, coarse_ref):
    group = 4
    width = weight_ref.shape[-1]
    channels = ext_ref.shape[1]

    def block(m, carry):
        most, least = carry
        total = None
        for tap in range(KW):
            start = pl.multiple_of((m * group + tap) * count, count)
            part = jnp.dot(
                ext_ref[pl.ds(start, group * count), :],
                weight_ref[:, :, 0, tap].reshape(channels, width),
                preferred_element_type=jnp.float32,
            )
            total = part if total is None else total + part
        for index in range(group):
            piece = total[index * count : (index + 1) * count]
            most = jnp.maximum(most, piece)
            least = jnp.minimum(least, piece)
        return most, least

    big = jnp.full((count, width), jnp.finfo(jnp.float32).max, jnp.float32)
    most, least = lax.fori_loop(0, POOL_B // group, block, (-big, big))
    bias = bias_ref[...]
    coarse_ref[...] = jnp.maximum(jax.nn.gelu(most + bias), jax.nn.gelu(least + bias)).astype(
        jnp.bfloat16
    )


def conv_stage(ext, weight, conv_bias):
    count = ext.shape[0] // (POOL_B + 4)
    ways, row_parts, column_parts, taps, depth, columns = weight.shape
    width = 256
    steps = columns // width
    return pl.pallas_call(
        functools.partial(conv_kernel, count),
        grid=(column_parts, steps),
        out_shape=jax.ShapeDtypeStruct((count, column_parts * columns), jnp.bfloat16),
        in_specs=[
            pl.BlockSpec(ext.shape, lambda b, n: (0, 0), pipeline_mode=pl.Buffered(1)),
            pl.BlockSpec(
                (ways, row_parts, 1, taps, depth, width), lambda b, n: (0, 0, b, 0, 0, n)
            ),
            pl.BlockSpec((1, width), lambda b, n: (0, b * steps + n)),
        ],
        out_specs=pl.BlockSpec((count, width), lambda b, n: (0, b * steps + n)),
        cost_estimate=pl.CostEstimate(
            flops=24_000_000_000, bytes_accessed=16_000_000, transcendentals=400_000
        ),
        name="conv_stage",
    )(ext, weight, conv_bias[None])


MESH = pl.DeviceIdType.MESH


UNITS = 12
GROUPS = 3


def encoder_kernel(
    tok_ref,
    stem_weight_ref,
    stem_bias_ref,
    gain_ref,
    conv_bias_ref,
    attn_gain_ref,
    conv_ref,
    query_ref,
    keyw_ref,
    valuew_ref,
    outw_ref,
    out_ref,
    coarse_ref,
    key_ref,
    value_ref,
    text_ref,
    hot_ref,
    shifted_ref,
    rows_ref,
    turn_ref,
    ext_ref,
    low_ref,
    high_ref,
    conv_full,
    proj_full,
    outw_full,
    pair_send,
    pair_recv,
    halo_send,
    halo_recv,
    local_sem,
    recv_sem,
    partner_sem,
    x_sem,
    y_sem,
    partner_send,
    own_sem,
    relay_sem,
):
    wide = out_ref.shape[1]
    members = lax.axis_size("seq")
    me = lax.axis_index("dp")
    place = lax.axis_index("seq")
    chip = me // 2
    core = me % 2
    chips = lax.axis_size("dp") // 2
    partner = (chip * 2 + 1 - core, place)
    count = tok_ref.shape[0]
    depth, width = conv_full.shape[5:]
    unit_rows = proj_full.shape[1] // UNITS
    kinds = GROUPS + 2
    split = HEADS * HEAD_K
    middle = split + HEAD_K

    along_x = place + 1 - 2 * (place % 2)
    along_y = place + 2 - 4 * (place // 2)
    across = 3 - place
    mine = (place % 2 + place // 2) % 2
    theirs = 1 - mine
    x_target = (me, along_x)
    y_target = (me, along_y)

    sources = (1 + chip % 2, (chip + 2) % chips, 3 - 3 * (chip % 2))
    inner = (chip > 0) & (chip < chips - 1)
    relays = (3 * (chip - 1), None, chips - 1 - chip)

    first = (place, 4 + mine)
    x_out = ((0, place, None), (1, along_y, 1), (2, 4 + mine, 0))
    y_out = ((0, place, None), (1, along_x, 0), (2, 4 + mine, 1))
    x_in = ((0, along_x, None), (1, across, 1), (2, 4 + theirs, 0))
    y_in = ((0, along_y, None), (1, across, 0), (2, 4 + theirs, 1))

    def full_of(kind):
        return (*(conv_full.at[group] for group in range(GROUPS)), proj_full, outw_full)[kind]

    def part(kind, way, pair, half=None):
        full = full_of(kind).at[way]
        if kind < GROUPS:
            return full.at[pair] if half is None else full.at[pair, half]
        unit = 2 * pair + (half or 0)
        span = 2 if half is None else 1
        return full.at[pl.ds(pl.multiple_of(unit * unit_rows, unit_rows), span * unit_rows)]

    def remote(ref, send_sem, recv, target):
        return pltpu.make_async_remote_copy(ref, ref, send_sem, recv, target, MESH)

    def arrived(ref, recv):
        remote(ref, x_sem.at[0], recv, partner).wait_recv()

    def to_partner(kind, ref):
        remote(ref, partner_send.at[kind], partner_sem.at[kind], partner).start()

    def own(kind, i):
        ref = part(kind, me, first[i])
        recv = recv_sem.at[kind, chip, i]

        @pl.when(chip < chips - 1)
        def _():
            remote(ref, own_sem.at[kind, 0], recv, (me + 2, place)).start()

        @pl.when(chip > 0)
        def _():
            remote(ref, own_sem.at[kind, 1], recv, (me - 2, place)).start()

        @pl.when(jnp.logical_not(inner))
        def _():
            far = 2 * (chips - 1 - chip) + core
            remote(ref, own_sem.at[kind, 2], recv, (far, place)).start()

    def plane_send(kind, origin, k):
        way = 2 * origin + core
        for base, out, sem, target in ((2, x_out, x_sem, x_target), (5, y_out, y_sem, y_target)):
            k, pair, half = out[k]
            recv = recv_sem.at[kind, origin, base + k]
            remote(part(kind, way, pair, half), sem.at[kind], recv, target).start()

    def z_step(kind, i, j):
        origin = sources[j]
        ref = part(kind, 2 * origin + core, first[i])
        recv = recv_sem.at[kind, origin, i]
        arrived(ref, recv)
        if relays[j] is not None:

            @pl.when(inner)
            def _():
                remote(ref, relay_sem.at[kind, j // 2], recv, (2 * relays[j] + core, place)).start()

        plane_send(kind, origin, 2 * i)
        to_partner(kind, ref)

    def plane_step(kind, i, j):
        origin = sources[j]
        way = 2 * origin + core
        for ks in ((0,), (1, 2))[i : i + 1]:
            for k in ks:
                for base, into in ((2, x_in), (5, y_in)):
                    _, pair, half = into[k]
                    ref = part(kind, way, pair, half)
                    arrived(ref, recv_sem.at[kind, origin, base + k])
                    to_partner(kind, ref)
        if i == 0:
            plane_send(kind, origin, 1)

    stream = [(kind, i) for kind in range(kinds) for i in range(2)]
    events = []
    for turn in range(len(stream) + 1):
        for j in (0, 2, 1):
            at = turn - (j == 1)
            if 0 <= at < len(stream) and not (turn == len(stream) and j != 1):
                events.append((at, j))
    def event(n):
        if n < 100:
            at, j = events[n]
            z_step(*stream[at], j)
            if at == 1 and j == 0:
                own(*stream[2])
            if at > 0 and j == 2 and at + 2 < len(stream):
                own(*stream[at + 2])
        else:
            at, j = events[n - 100]
            plane_step(*stream[at], j)

    def run(*some):
        for n in some:
            event(n)

    def plane(*some):
        return [100 + n for n in some]

    def event_of(number, lists):
        for index, some in enumerate(lists):

            @pl.when(number == index)
            def _():
                run(*some)

    def local_copies(kind):
        if kind < GROUPS:
            for pair in range(UNITS // 2):
                for half in range(2):
                    rows = pl.ds(pair * depth, depth)
                    columns = pl.ds((2 * kind + half) * width, width)
                    yield conv_ref.at[:, rows, columns], part(kind, me, pair, half)
        elif kind == GROUPS:
            yield query_ref, proj_full.at[me, :, pl.ds(0, split)]
            yield keyw_ref, proj_full.at[me, :, pl.ds(split, HEAD_K)]
            yield valuew_ref, proj_full.at[me, :, pl.ds(middle, HEAD_V)]
        else:
            yield outw_ref, outw_full.at[me]

    def local_start(kind):
        for a, b in local_copies(kind):
            pltpu.make_async_copy(a, b, local_sem.at[kind]).start()

    def local_wait(kind):
        whole = full_of(kind).at[me]
        pltpu.make_async_copy(whole, whole, local_sem.at[kind]).wait()

    def own_partner(kind):
        to_partner(kind, full_of(kind).at[me])

    barrier = pltpu.get_barrier_semaphore()
    pl.semaphore_signal(barrier, inc=1, device_id=partner, device_id_type=MESH)
    for turn in (1, chips - 1):
        neighbour = (chip + turn) % chips * 2 + core
        pl.semaphore_signal(barrier, inc=1, device_id=(neighbour, place), device_id_type=MESH)
    for turn in range(1, members):
        pl.semaphore_signal(
            barrier, inc=1, device_id=(me, (place + turn) % members), device_id_type=MESH
        )
    local_start(0)
    local_wait(0)
    pl.semaphore_wait(barrier, members + 2)

    right = (place + 1) % members
    left = (place + members - 1) % members
    halo = [
        pltpu.make_async_remote_copy(
            tok_ref.at[count - 8 : count], low_ref, halo_send.at[0], halo_recv.at[0], (me, right), MESH
        ),
        pltpu.make_async_remote_copy(
            tok_ref.at[0:8], high_ref, halo_send.at[1], halo_recv.at[1], (me, left), MESH
        ),
    ]
    for copy in halo:
        copy.start()
    own(0, 0)
    stem_shift(stem_weight_ref, shifted_ref)
    own(0, 1)
    own_partner(0)
    for kind in range(1, kinds):
        local_start(kind)
    stem_inside(tok_ref, text_ref, hot_ref)

    half_dim = HEAD_K // 2
    lane = lax.broadcasted_iota(jnp.int32, (count, HEAD_K), 1)
    step = lane % half_dim
    freqs = jnp.exp(step.astype(jnp.float32) * (-math.log(10000.0) / half_dim))
    position = place * count + lax.broadcasted_iota(jnp.int32, (count, HEAD_K), 0)
    angles = position.astype(jnp.float32) * freqs
    turn_ref[0] = jnp.cos(angles)
    sine = jnp.sin(angles)
    turn_ref[1] = jnp.where(lane < half_dim, -sine, sine)

    def outside():
        for copy in halo:
            copy.wait()
        low = jnp.where(place > 0, low_ref[7:8], 0)
        high = jnp.where(place < members - 1, high_ref[0:1], 0)
        stem_outside(column_of(low, GROUP), column_of(high, GROUP), text_ref, hot_ref)

    def loaded():
        for kind in range(1, kinds):
            local_wait(kind)
        own_partner(1)

    def passed():
        for kind in range(2, kinds):
            own_partner(kind)

    inner_events = [[n, *plane(*range(max(n - 2, 0), n - 1))] for n in range(7)]
    inner_events += [[7, *plane(5), 8, *plane(6)], []]
    outer_events = inner_events[:5]
    outer_events += [[7, *plane(3)], [*plane(4)], [5, 6], [*plane(7), 8, 9]]

    def stem_round(r, nothing):
        def block(step, nothing):
            j = (step + 1) % (POOL_B + 1)
            stem_block(j, stem_bias_ref, gain_ref, ext_ref, hot_ref, shifted_ref, rows_ref)
            return nothing

        lax.fori_loop(2 * r, 2 * r + 2 - r // 8, block, 0)
        pl.when(r == 1)(loaded)
        pl.when(r == 3)(outside)
        pl.when(r == 5)(passed)

        @pl.when(inner)
        def _():
            event_of(r, inner_events)

        @pl.when(jnp.logical_not(inner))
        def _():
            event_of(r, outer_events)

        return nothing

    lax.fori_loop(0, POOL_B // 2 + 1, stem_round, 0)
    stem_edges(place, members - 1, ext_ref, rows_ref)

    group = 8
    channels = ext_ref.shape[1]
    big = jnp.full((count, width), jnp.finfo(jnp.float32).max, jnp.float32)

    def conv_panel(turn, half, after):
        weight_ref = conv_full.at[turn, :, :, half]

        def block(m, carry):
            most, least = carry
            weight = jnp.concatenate(
                [weight_ref[:, :, tap].reshape(channels, width) for tap in range(KW)], axis=0
            )
            rows = jnp.concatenate(
                [
                    ext_ref[pl.ds(pl.multiple_of((m * group + tap) * count, count), group * count), :]
                    for tap in range(KW)
                ],
                axis=1,
            )
            total = jnp.dot(rows, weight, preferred_element_type=jnp.float32)
            for index in range(group):
                piece = total[index * count : (index + 1) * count]
                most = jnp.maximum(most, piece)
                least = jnp.minimum(least, piece)
            after(m)
            return most, least

        most, least = lax.fori_loop(0, POOL_B // group, block, (-big, big))
        at = pl.multiple_of((2 * turn + half) * width, width)
        bias = conv_bias_ref[pl.ds(at, width)].reshape(1, width)
        coarse_ref[:, pl.ds(at, width)] = jnp.maximum(
            jax.nn.gelu(most + bias), jax.nn.gelu(least + bias)
        ).astype(jnp.bfloat16)

    late_events = [
        [10, 11, *plane(8)],
        [12, 13, *plane(9)],
        [14, *plane(10, 11)],
        [15, *plane(12)],
        [17, 18, *plane(14)],
        [19, *plane(15, 16)],
        [20, 21, *plane(17)],
        [22, *plane(18)],
        [24, *plane(20, 21)],
        [25, 26, *plane(22)],
        [27, *plane(23, 24)],
        [28, *plane(25)],
    ]
    between = [[], [16, *plane(13)], [23, *plane(19)]]
    pl.when(inner)(lambda: run(9, *plane(7)))
    pl.when(jnp.logical_not(inner))(lambda: run(*plane(5, 6)))

    def conv_turn(t, nothing):
        for turn in range(GROUPS):

            @pl.when(t == 2 * turn)
            def _():
                run(*between[turn])
                arrived(conv_full.at[turn, pl.ds(0, chips)], partner_sem.at[turn])

        conv_panel(t // 2, t % 2, lambda m: event_of(POOL_B // group * t + m, late_events))
        return nothing

    lax.fori_loop(0, 2 * GROUPS, conv_turn, 0)
    arrived(proj_full.at[pl.ds(0, chips)], partner_sem.at[GROUPS])

    def weight(begin, end):
        return proj_full[:, :, begin:end].reshape(wide, end - begin)

    def turned(head):
        return (head * turn_ref[0] + pltpu.roll(head, HEAD_K // 2, 1) * turn_ref[1]).astype(jnp.bfloat16)

    hidden = rms_scale(coarse_ref[...].astype(jnp.float32), attn_gain_ref[...].reshape(1, -1)).astype(
        jnp.bfloat16
    )
    key_ref[place] = turned(
        jnp.dot(hidden, weight(split, middle), preferred_element_type=jnp.float32)
    )
    value_ref[place] = jnp.dot(
        hidden, weight(middle, middle + HEAD_V), preferred_element_type=jnp.float32
    ).astype(jnp.bfloat16)
    pairs = []
    for turn in range(1, members):
        for index, ref in enumerate((key_ref, value_ref)):
            copy = pltpu.make_async_remote_copy(
                ref.at[place],
                ref.at[place],
                pair_send.at[index, turn],
                pair_recv.at[index, place],
                (me, (place + turn) % members),
                MESH,
            )
            copy.start()
            pairs.append(copy)
    query = jnp.dot(hidden, weight(0, split), preferred_element_type=jnp.float32)
    run(*plane(26), 29, *plane(27, 28))
    for turn in range(1, members):
        spot = (place + turn) % members
        for index, ref in enumerate((key_ref, value_ref)):
            arrived(ref.at[spot], pair_recv.at[index, spot])
    keys = key_ref[...].reshape(members * count, HEAD_K)
    values = value_ref[...].reshape(members * count, HEAD_V)
    mixes = []
    for head in range(HEADS):
        scores = lax.dot_general(
            turned(query[:, head * HEAD_K : (head + 1) * HEAD_K]),
            keys,
            (((1,), (1,)), ((), ())),
            preferred_element_type=jnp.float32,
        ) * HEAD_K ** (-0.5)
        raised = jnp.exp(scores - jnp.max(scores, axis=-1, keepdims=True))
        weights = (raised / jnp.sum(raised, axis=-1, keepdims=True)).astype(jnp.bfloat16)
        mixes.append(
            jnp.dot(weights, values, preferred_element_type=jnp.float32).astype(jnp.bfloat16)
        )
    run(*plane(29))
    arrived(outw_full.at[pl.ds(0, chips)], partner_sem.at[GROUPS + 1])
    total = coarse_ref[...].astype(jnp.float32)
    for head in range(HEADS):
        total = total + jnp.dot(mixes[head], outw_full[head], preferred_element_type=jnp.float32)
    out_ref[...] = total.astype(jnp.bfloat16)
    for copy in pairs:
        copy.wait_send()
    for kind in range(kinds):
        whole = full_of(kind).at[0]
        remote(whole, x_sem.at[kind], recv_sem.at[0, 0, 0], x_target).wait_send()
        remote(whole, y_sem.at[kind], recv_sem.at[0, 0, 0], y_target).wait_send()
        every = full_of(kind).at[pl.ds(0, chips)]
        remote(every, partner_send.at[kind], recv_sem.at[0, 0, 0], partner).wait_send()
        ref = full_of(kind).at[0, pl.ds(0, 2 if kind < GROUPS else 4 * unit_rows)]

        @pl.when(chip < chips - 1)
        def _():
            remote(ref, own_sem.at[kind, 0], recv_sem.at[0, 0, 0], partner).wait_send()

        @pl.when(chip > 0)
        def _():
            remote(ref, own_sem.at[kind, 1], recv_sem.at[0, 0, 0], partner).wait_send()

        @pl.when(jnp.logical_not(inner))
        def _():
            remote(ref, own_sem.at[kind, 2], recv_sem.at[0, 0, 0], partner).wait_send()

        @pl.when(inner)
        def _():
            for index in range(2):
                remote(ref, relay_sem.at[kind, index], recv_sem.at[0, 0, 0], partner).wait_send()


def fits(ways, members, conv_weight, w_query, w_out):
    taps, depth, columns = conv_weight.shape
    rows = w_out.shape[0]
    return (
        ways == 8
        and members == 4
        and columns == 2 * GROUPS * 256
        and depth == UNITS // 2 * 16
        and rows == HEAD_V
        and HEADS == ways
        and rows % (16 * UNITS) == 0
    )


def encoder_stage(
    tokens, stem_weight, vectors, conv_weight, w_query, w_key, w_value, w_out
):
    count = tokens.shape[0]
    channels = stem_weight.shape[1]
    taps, depth, columns = conv_weight.shape
    rows = w_out.shape[0]
    ways = lax.axis_size("dp")
    members = lax.axis_size("seq")
    chips = ways // 2
    vmem = pl.BlockSpec(memory_space=pltpu.VMEM)
    hbm = pl.BlockSpec(memory_space=pl.ANY)
    dma = pltpu.SemaphoreType.DMA
    kinds = GROUPS + 2
    return pl.pallas_call(
        encoder_kernel,
        out_shape=jax.ShapeDtypeStruct((count, columns), jnp.bfloat16),
        in_specs=[vmem] * 6 + [hbm] * 5,
        out_specs=vmem,
        scratch_shapes=[
            pltpu.VMEM((count, columns), jnp.bfloat16),
            pltpu.VMEM((members, count, HEAD_K), jnp.bfloat16),
            pltpu.VMEM((members, count, HEAD_V), jnp.bfloat16),
            pltpu.VMEM((GROUP + 2 * SPAN, count), jnp.float32),
            pltpu.VMEM((POOL_B + 1, count, GROUP), jnp.bfloat16),
            pltpu.VMEM((POOL_A, GROUP, channels), jnp.bfloat16),
            pltpu.VMEM((count, channels), jnp.float32),
            pltpu.VMEM((2, count, HEAD_K), jnp.float32),
            pltpu.VMEM(((POOL_B + 4) * count, channels), jnp.bfloat16),
            pltpu.VMEM((8, GROUP), jnp.int32),
            pltpu.VMEM((8, GROUP), jnp.int32),
            pltpu.VMEM(
                (GROUPS, ways, UNITS // 2, 2, taps, depth // 6, columns // (2 * GROUPS)), jnp.bfloat16
            ),
            pltpu.VMEM((ways, rows, HEADS * HEAD_K + HEAD_K + HEAD_V), jnp.bfloat16),
            pltpu.VMEM((ways, rows, columns), jnp.bfloat16),
            dma((2, members)),
            dma((2, members)),
            dma((2,)),
            dma((2,)),
            dma((kinds,)),
            dma((kinds, chips, 8)),
            dma((kinds,)),
            dma((kinds,)),
            dma((kinds,)),
            dma((kinds,)),
            dma((kinds, 3)),
            dma((kinds, 2)),
        ],
        compiler_params=pltpu.CompilerParams(
            collective_id=0, has_side_effects=True, vmem_limit_bytes=40 * 2**20
        ),
        name="encoder_stage",
    )(*(pltpu.with_memory_space_constraint(x, pltpu.HBM) for x in (tokens, stem_weight, *vectors, conv_weight, w_query, w_key, w_value, w_out)))


def gather_conv(conv_weight):
    taps, depth, columns = conv_weight.shape
    members = lax.axis_size("seq")
    place = lax.axis_index("seq")
    for row_parts in (2, 1, 3):
        column_parts = members // row_parts
        if members % row_parts or depth % (16 * row_parts) or columns % (256 * column_parts):
            continue
        depth_part = depth // row_parts
        column_part = columns // column_parts
        piece = lax.dynamic_slice(
            conv_weight,
            (0, place // column_parts * depth_part, place % column_parts * column_part),
            (taps, depth_part, column_part),
        )
        full = lax.all_gather(piece, ("dp", "seq"), axis=0, tiled=False)
        return full.reshape(-1, row_parts, column_parts, taps, depth_part, column_part)
    full = lax.all_gather(conv_weight, "dp", axis=0, tiled=False)
    return full[:, None, None]


def gather_rows(weight):
    members = lax.axis_size("seq")
    rows = weight.shape[0] // members
    piece = lax.dynamic_slice_in_dim(weight, lax.axis_index("seq") * rows, rows, axis=0)
    return lax.all_gather(piece, ("dp", "seq"), axis=0, tiled=True)


def body(
    tokens,
    stem_weight,
    stem_bias,
    conv_gain,
    conv_weight,
    conv_bias,
    attn_gain,
    w_query,
    w_key,
    w_value,
    w_out,
):
    seq_local = tokens.shape[1]
    rows_att = seq_local // GROUP
    tokens = tokens.reshape(rows_att, GROUP)
    size = lax.axis_size("seq")
    rows = w_out.shape[0]
    split = HEADS * HEAD_K
    if fits(lax.axis_size("dp"), size, conv_weight, w_query, w_out):
        return encoder_stage(
            tokens,
            stem_weight,
            [stem_bias, conv_gain, conv_bias, attn_gain],
            conv_weight,
            w_query,
            w_key,
            w_value,
            w_out,
        )[None]
    else:
        full_conv = gather_conv(conv_weight)
        projections = gather_rows(jnp.concatenate([w_query, w_key, w_value], axis=1))
        first_rows = projections[:, : split + HEAD_K]
        value_rows = projections[:, split + HEAD_K :]
        full_out = gather_rows(w_out)
        forward = [(i, i + 1) for i in range(size - 1)]
        backward = [(i + 1, i) for i in range(size - 1)]
        low = lax.ppermute(tokens[-1:], "seq", forward)
        high = lax.ppermute(tokens[:1], "seq", backward)
        ext = stem_stage(tokens, low, high, stem_weight, stem_bias, conv_gain)
        coarse = conv_stage(ext, full_conv, conv_bias)
    residual = coarse.astype(jnp.float32)
    hidden = rms_scale(residual, attn_gain).astype(jnp.bfloat16)
    projected = jnp.dot(hidden, first_rows, preferred_element_type=jnp.float32)
    query = projected[:, :split]
    keys = projected[:, split:]
    values = jnp.dot(hidden, value_rows, preferred_element_type=jnp.float32)
    half_dim = HEAD_K // 2
    freqs = 10000.0 ** (-jnp.arange(half_dim, dtype=jnp.float32) / half_dim)
    positions = lax.axis_index("seq") * rows_att + jnp.arange(rows_att, dtype=jnp.int32)
    angles = positions.astype(jnp.float32)[:, None] * freqs[None, :]
    query = rotate(query.reshape(rows_att, HEADS, HEAD_K), angles[:, None, :]).astype(jnp.bfloat16)
    keys = rotate(keys, angles).astype(jnp.bfloat16)
    pair = jnp.concatenate([keys, values.astype(jnp.bfloat16)], axis=1)
    pair = lax.all_gather(pair, "seq", axis=0, tiled=True)
    keys_all, values_all = pair[:, :HEAD_K], pair[:, HEAD_K:]
    scores = jnp.einsum(
        "rhd,kd->hrk", query, keys_all, preferred_element_type=jnp.float32
    ) * HEAD_K ** (-0.5)
    weights = jax.nn.softmax(scores, axis=-1).astype(jnp.bfloat16)
    mixed = jnp.einsum(
        "hrk,kd->rhd", weights, values_all, preferred_element_type=jnp.float32
    ).astype(jnp.bfloat16)
    mixed = mixed.reshape(rows_att, HEADS * HEAD_V)
    out = jnp.dot(mixed, full_out, preferred_element_type=jnp.float32)
    return (residual + out).astype(jnp.bfloat16)[None]


def solution(mesh):
    in_specs = (
        P("dp", "seq"),
        P(),
        P(),
        P(),
        P(None, "dp", None),
        P(),
        P(),
        P("dp", None),
        P("dp", None),
        P("dp", None),
        P("dp", None),
    )
    out_specs = P("dp", "seq", None)
    return jax.shard_map(body, mesh=mesh, in_specs=in_specs, out_specs=out_specs, check_vma=False)
```
